32 devices in a mesh: gx: 4 (over y, x), gy: 4 (over z), gz: 2 (over core).
Axes of the slice: x: 2, y: 2, z: 4, core: 2. Of those that a mesh axis runs over, the one named last changes fastest.
Arguments:
- tile_coords: int32 [3, 512], P(None, ('gx', 'gy', 'gz')), may hold values from 0 to 15, as said below
- owner_map: int32 [512], replicated, may hold values from 0 to 511, as said below
- bin_tile: int32 [1856], P(('gx', 'gy', 'gz')), may hold values from 0 to 511, as said below
- bin_count: int32 [1856], P(('gx', 'gy', 'gz')), may hold values from 0 to 2048, as said below
- part_cell: int32 [1856, 2048], P(('gx', 'gy', 'gz')), may hold values from 0 to 511
- part_offset: float32 [1856, 3, 2048], P(('gx', 'gy', 'gz')), may hold values from -0.5 to 0.5
- part_velocity: float32 [1856, 3, 2048], P(('gx', 'gy', 'gz')), may hold values from -5 to 5
- part_affine: float32 [1856, 9, 2048], P(('gx', 'gy', 'gz')), may hold values from -5 to 5
- part_mass: float32 [1856, 2048], P(('gx', 'gy', 'gz')), may hold values from 0.5 to 2
Outputs:
- grid_velocity: float32 [3, 262144], P(None, ('gx', 'gy', 'gz'))
- pressure: float32 [262144], P(('gx', 'gy', 'gz'))
- particle_velocity: float32 [1856, 3, 2048], P(('gx', 'gy', 'gz'))
The draws below stay inside these ranges and needn't reach their ends.
Inputs may be any that keep to these rules, and one draw needn't show every extreme that they name: `tile_coords`: storage slot s lies on device s // 16 (device index over gx, gy, gz, slowest first). Coordinates are distinct; an active tile that shares a face with a tile stored on a device is stored on the same device or on one whose index differs by one along one mesh axis. `owner_map`: A permutation of the storage slots. `bin_tile`: the 58 bins of a device are first 32 bins whose tiles it stores itself, then 1 bins for each of the 26 offsets (dx, dy, dz) in -1..1 other than (0, 0, 0), in the order dx slowest, dz fastest, whose tiles are stored on the device at that offset of mesh indices. Bins of an offset that leads outside the mesh name some tile and hold no particles. The first bin_count slots of a bin hold its particles. Every device has a bin holding 2048.
All inputs are finite; a program needn't handle non-finite values.
Results may differ from the reference program's by a relative error of at most 0.0024.
The reference program's roundings to bfloat16 on the way count: a program that leaves them out, or rounds other values in their place, can miss the bound.
Values sent between devices are 32-bit elements; how exact they have to be, the bound alone decides.
A program may use at most 128 MiB of HBM per device.

```python
import math
import jax
import jax.numpy as jnp
import numpy as np
from jax import lax

TILE = 8
HOME = 4
TPD = 16
SELF_BINS = 32
NBR_BINS = 1
PPT = 2048
SWEEPS = 4
CELLS = 512
BINS = 1856
N_GX = 4
N_GY = 4
N_GZ = 2


neighbour_steps = [(along_x, along_y, along_z) for along_x in (-1, 0, 1) for along_y in (-1, 0, 1) for along_z in (-1, 0, 1) if (along_x, along_y, along_z) != (0, 0, 0)]


def world_layout(key):
    base_key = jax.random.fold_in(key, 4242)
    device_total = N_GX * N_GY * N_GZ
    grid_points = np.array([(along_x, along_y, along_z) for along_x in range(HOME) for along_y in range(HOME) for along_z in range(HOME)], dtype=np.int32)
    is_inner = np.all((grid_points >= 1) & (grid_points <= HOME - 2), axis=1)
    interior = jnp.asarray(grid_points[is_inner])
    surface = jnp.asarray(grid_points[~is_inner])
    inner_total = int(is_inner.sum())
    surface_total = grid_points.shape[0] - inner_total
    inner_order = jax.vmap(lambda subkey: jax.random.permutation(subkey, inner_total))(jax.random.split(jax.random.fold_in(base_key, 1), device_total))
    surface_order = jax.vmap(lambda subkey: jax.random.permutation(subkey, surface_total))(jax.random.split(jax.random.fold_in(base_key, 2), device_total))[:, :TPD - inner_total]
    local_places = jnp.concatenate([interior[inner_order], surface[surface_order]], axis=1)
    devices = jnp.arange(device_total, dtype=jnp.int32)
    placing = jnp.stack([devices // (N_GY * N_GZ), devices // N_GZ % N_GY, devices % N_GZ], axis=1)
    home_coords = placing[:, None, :] * HOME + local_places
    swap_axis = jax.random.randint(jax.random.fold_in(base_key, 3), (), 0, 3)
    parity = jax.random.randint(jax.random.fold_in(base_key, 4), (), 0, 2)
    chosen = jax.random.permutation(jax.random.fold_in(base_key, 5), inner_total)[:2]
    extents = jnp.array([N_GX, N_GY, N_GZ], dtype=jnp.int32)
    strides = jnp.array([N_GY * N_GZ, N_GZ, 1], dtype=jnp.int32)
    along_swap = jnp.take(placing, swap_axis, axis=1)
    swap_limit = extents[swap_axis]
    shifted = along_swap - parity
    upward = (shifted >= 0) & (shifted % 2 == 0) & (along_swap + 1 < swap_limit)
    downward = (shifted >= 0) & (shifted % 2 == 1)
    partner = devices + jnp.where(upward, 1, jnp.where(downward, -1, 0)) * strides[swap_axis]
    shuffles = jax.vmap(lambda subkey: jax.random.permutation(subkey, TPD))(jax.random.split(jax.random.fold_in(base_key, 8), device_total)).astype(jnp.int32)
    home_index = shuffles
    moving = (home_index == chosen[0]) | (home_index == chosen[1])
    holder = jnp.where(moving, partner[:, None], devices[:, None])
    stored = (holder * TPD + home_index).reshape(-1).astype(jnp.int32)
    slot_total = device_total * TPD
    owner = jnp.zeros((slot_total,), jnp.int32).at[stored].set(jnp.arange(slot_total, dtype=jnp.int32))
    coords = jnp.transpose(home_coords.reshape(-1, 3)[stored]).astype(jnp.int32)
    tile_order = jax.vmap(lambda subkey: jax.random.permutation(subkey, TPD))(jax.random.split(jax.random.fold_in(base_key, 6), device_total))
    self_pick = tile_order[:, jnp.arange(SELF_BINS, dtype=jnp.int32) % TPD]
    offsets = jnp.array(neighbour_steps, dtype=jnp.int32)
    target = placing[:, None, :] + offsets[None, :, :]
    inside = jnp.all((target >= 0) & (target < extents[None, None, :]), axis=2)
    target_dev = jnp.where(inside, (target[:, :, 0] * N_GY + target[:, :, 1]) * N_GZ + target[:, :, 2], devices[:, None])
    near_pick = jax.random.randint(jax.random.fold_in(base_key, 7), (device_total, 26, NBR_BINS), 0, TPD)
    slot_all = jnp.concatenate([devices[:, None] * TPD + self_pick, (target_dev[:, :, None] * TPD + near_pick).reshape(device_total, 26 * NBR_BINS)], axis=1)
    bin_tiles = stored[slot_all].reshape(-1).astype(jnp.int32)
    bins_dev = SELF_BINS + 26 * NBR_BINS
    counts = jax.random.randint(jax.random.fold_in(base_key, 9), (device_total, bins_dev), PPT * 3 // 5, PPT + 1)
    full_bin = jax.random.randint(jax.random.fold_in(base_key, 10), (device_total, 1), 0, SELF_BINS)
    counts = jnp.where(jnp.arange(bins_dev, dtype=jnp.int32)[None, :] == full_bin, PPT, counts)
    valid_bins = jnp.concatenate([jnp.ones((device_total, SELF_BINS), dtype=bool), jnp.repeat(inside, NBR_BINS, axis=1)], axis=1)
    counts = jnp.where(valid_bins, counts, 0).reshape(-1).astype(jnp.int32)
    return (coords, owner, bin_tiles, counts)


def draw_tile_coords(key, part):
    return world_layout(key)[0]


def draw_owner_map(key, part):
    return world_layout(key)[1]


def draw_bin_tile(key, part):
    return world_layout(key)[2]


def draw_bin_count(key, part):
    return world_layout(key)[3]


def with_ends(result, key, least, high):
    longest = result.shape.index(max(result.shape))
    spots = []
    for shift in (0, 1):
        where = [jax.random.randint(jax.random.fold_in(key, axis), (), 0, length) for axis, length in enumerate(result.shape)]
        where[longest] = (where[longest] + shift) % result.shape[longest]
        spots.append(tuple(where))
    return result.at[spots[0]].set(least).at[spots[1]].set(high)


def block_levels(key, dims, pieces, least, largest):
    gain, own = 1.0, jax.random.fold_in(key, 6)
    for position, shards_of in pieces:
        draws = jnp.exp(jax.random.uniform(jax.random.fold_in(own, position), (shards_of,), jnp.float32, least / len(pieces), largest / len(pieces)))
        gain = gain * jnp.repeat(draws, dims[position] // shards_of).reshape([-1 if axis == position else 1 for axis in range(len(dims))])
    return gain


def scatter_about(rng, shape, deviation, most, pieces=(), kind=jnp.bfloat16):
    values = jax.random.normal(rng, shape, jnp.float32) * deviation
    if len(pieces) > 0:
        values = block_levels(rng, shape, pieces, -0.22, 0.18) * values
    return jnp.clip(values, min=-most, max=most).astype(kind)


def setup_inputs(seed: int = 0) -> dict:
    key_of = jax.random.split(jax.random.key(seed), 10)
    return {
        "tile_coords": draw_tile_coords(jax.random.fold_in(key_of[9], 71), 0),
        "owner_map": draw_owner_map(jax.random.fold_in(key_of[9], 71), 0),
        "bin_tile": draw_bin_tile(jax.random.fold_in(key_of[9], 71), 0),
        "bin_count": draw_bin_count(jax.random.fold_in(key_of[9], 71), 0),
        "part_cell": with_ends(jax.random.randint(key_of[4], (BINS, PPT), 0, CELLS), jax.random.fold_in(key_of[4], 1), 0, CELLS - 1).astype(jnp.int32),
        "part_offset": jnp.clip(jax.random.uniform(key_of[5], (BINS, 3, PPT), jnp.float32, -0.5, 0.5) * block_levels(key_of[5], (BINS, 3, PPT), ((0, 32),), -0.4, 0.0), -0.5, 0.5),
        "part_velocity": scatter_about(key_of[6], (BINS, 3, PPT), 1.0, 5.0, ((0, 32),), jnp.float32),
        "part_affine": scatter_about(key_of[7], (BINS, 9, PPT), 1.0, 5.0, ((0, 32),), jnp.float32),
        "part_mass": jnp.clip(jnp.exp(math.log(2.0) - 1.3862944 * jax.random.uniform(key_of[8], (BINS, PPT), jnp.float32) ** block_levels(key_of[8], (BINS, PPT), ((0, 32),), -0.2, 0.2)), 0.5, 2.0),
    }


gravity_step = 0.5
face_steps = [(1, 0, 0), (-1, 0, 0), (0, 1, 0), (0, -1, 0), (0, 0, 1), (0, 0, -1)]


def deposits(offsets, velocity, affine, masses, living):
    moments = []
    for component in range(3):
        drift_part = velocity[:, component] - (affine[:, 3 * component] * offsets[:, 0] + affine[:, 3 * component + 1] * offsets[:, 1] + affine[:, 3 * component + 2] * offsets[:, 2])
        moments.append(masses * drift_part)
    stacked = jnp.stack([masses] + moments, axis=1)
    return jnp.where(living[:, None, :], stacked, 0.0).astype(jnp.bfloat16)


def lattice_rows(tile_coords):
    extent_x = HOME * N_GX
    extent_y = HOME * N_GY
    extent_z = HOME * N_GZ
    tile_total = tile_coords.shape[1]
    linear = (tile_coords[0] * extent_y + tile_coords[1]) * extent_z + tile_coords[2]
    lookup = jnp.full((extent_x * extent_y * extent_z,), -1, jnp.int32).at[linear].set(jnp.arange(tile_total, dtype=jnp.int32))
    listing = []
    for relative in face_steps:
        shifted_coord = [tile_coords[number] + relative[number] for number in range(3)]
        inside = (shifted_coord[0] >= 0) & (shifted_coord[0] < extent_x) & (shifted_coord[1] >= 0) & (shifted_coord[1] < extent_y) & (shifted_coord[2] >= 0) & (shifted_coord[2] < extent_z)
        address = (jnp.clip(shifted_coord[0], 0, extent_x - 1) * extent_y + jnp.clip(shifted_coord[1], 0, extent_y - 1)) * extent_z + jnp.clip(shifted_coord[2], 0, extent_z - 1)
        listing.append(jnp.where(inside, lookup[address.astype(jnp.int32)], -1).astype(jnp.int32))
    return jnp.stack(listing, axis=1)


def export_faces(values):
    return jnp.stack([values[:, 0], values[:, -1], values[:, :, 0], values[:, :, -1], values[:, :, :, 0], values[:, :, :, -1]], axis=1)


def component_faces(velocity):
    return jnp.stack([velocity[:, 0, 0], velocity[:, 0, -1], velocity[:, 1, :, 0], velocity[:, 1, :, -1], velocity[:, 2, :, :, 0], velocity[:, 2, :, :, -1]], axis=1)


def beside(values, face_table, neighbour_rows, facing):
    direction = facing // 2
    chosen_rows = neighbour_rows[:, facing]
    ghost_layer = jnp.where((chosen_rows >= 0)[:, None, None], face_table[jnp.maximum(chosen_rows, 0), facing], 0.0)
    ghost_layer = jnp.expand_dims(ghost_layer, direction + 1)
    extent = values.shape[1]
    if facing % 2 == 0:
        return jnp.concatenate([lax.slice_in_dim(values, 1, extent, axis=direction + 1), ghost_layer], axis=direction + 1)
    return jnp.concatenate([ghost_layer, lax.slice_in_dim(values, 0, extent - 1, axis=direction + 1)], axis=direction + 1)


def beside_all(values, face_table, neighbour_rows):
    summed = beside(values, face_table, neighbour_rows, 0)
    for facing in range(1, 6):
        summed = summed + beside(values, face_table, neighbour_rows, facing)
    return summed


def reference(tile_coords, owner_map, bin_tile, bin_count, part_cell, part_offset, part_velocity, part_affine, part_mass):
    plane_cells = TILE * TILE
    total_cells = TILE * plane_cells
    tile_total = tile_coords.shape[1]
    owner_slots = owner_map[bin_tile]
    living = lax.broadcasted_iota(jnp.int32, part_cell.shape, 1) < bin_count[:, None]
    amounts = deposits(part_offset, part_velocity, part_affine, part_mass, living)
    places = (owner_slots[:, None] * total_cells + part_cell).astype(jnp.int32)
    spread = jnp.transpose(amounts.astype(jnp.float32), (1, 0, 2)).reshape(4, -1)
    grid_sums = jnp.zeros((4, tile_total * total_cells), jnp.float32).at[:, places.reshape(-1)].add(spread)
    totals = jnp.transpose(grid_sums.reshape(4, tile_total, TILE, TILE, TILE), (1, 0, 2, 3, 4))
    neighbour_rows = lattice_rows(tile_coords)
    masses = totals[:, 0]
    fluid_mask = masses > 0.0
    safe_mass = jnp.where(fluid_mask, masses, 1.0)
    velocity = jnp.where(fluid_mask[:, None], totals[:, 1:] / safe_mass[:, None], 0.0)
    upward = jnp.array([0.0, 1.0, 0.0], dtype=jnp.float32)
    velocity = velocity - gravity_step * fluid_mask.astype(jnp.float32)[:, None] * upward[None, :, None, None, None]
    velocity_table = component_faces(velocity)
    diverge = 0.5 * (beside(velocity[:, 0], velocity_table, neighbour_rows, 0) - beside(velocity[:, 0], velocity_table, neighbour_rows, 1))
    diverge = diverge + 0.5 * (beside(velocity[:, 1], velocity_table, neighbour_rows, 2) - beside(velocity[:, 1], velocity_table, neighbour_rows, 3))
    diverge = diverge + 0.5 * (beside(velocity[:, 2], velocity_table, neighbour_rows, 4) - beside(velocity[:, 2], velocity_table, neighbour_rows, 5))
    pressure = jnp.zeros_like(masses)
    for sweep_number in range(SWEEPS):
        face_table = export_faces(pressure)
        pressure = jnp.where(fluid_mask, (beside_all(pressure, face_table, neighbour_rows) - diverge) / 6.0, 0.0)
    face_table = export_faces(pressure)
    gradient = jnp.stack([0.5 * (beside(pressure, face_table, neighbour_rows, 2 * component) - beside(pressure, face_table, neighbour_rows, 2 * component + 1)) for component in range(3)], axis=1)
    velocity = jnp.where(fluid_mask[:, None], velocity - gradient, 0.0)
    flat_velocity = jnp.transpose(velocity, (1, 0, 2, 3, 4)).reshape(3, tile_total * total_cells)
    sampled = jnp.transpose(flat_velocity[:, places], (1, 0, 2))
    particle_velocity = jnp.where(living[:, None, :], sampled, 0.0)
    return flat_velocity, pressure.reshape(-1), particle_velocity
```

```python
import functools

import jax
import jax.numpy as jnp
from jax import lax
from jax.experimental import pallas as pl
from jax.experimental.pallas import tpu as pltpu
from jax.sharding import PartitionSpec as P

TILE = 8
SELF_BINS = 32
SWEEPS = 4
CELLS = TILE * TILE * TILE
LANES = 128
GROUPS = CELLS // LANES
QROWS = 4 * GROUPS
BLOCK = QROWS + 8
STEP_BINS = 8
GRAVITY = 0.5
AXES = ("gx", "gy", "gz")
MESH = pl.DeviceIdType.MESH

OFFSETS = [
    (x, y, z)
    for x in (-1, 0, 1)
    for y in (-1, 0, 1)
    for z in (-1, 0, 1)
    if (x, y, z) != (0, 0, 0)
]
FACES = [(1, 0, 0), (-1, 0, 0), (0, 1, 0), (0, -1, 0), (0, 0, 1), (0, 0, -1)]


def lower_hot(cell_row):
    points = cell_row.shape[1]
    low = (cell_row & (LANES - 1)).astype(jnp.float32).astype(jnp.bfloat16)
    rows = lax.broadcasted_iota(jnp.int32, (LANES, points), 0)
    rows = rows.astype(jnp.float32).astype(jnp.bfloat16)
    return jnp.where(rows == low, jnp.bfloat16(1), jnp.bfloat16(0))


def upper_row(cell_row, count):
    lane = lax.broadcasted_iota(jnp.int32, cell_row.shape, 1)
    return jnp.where(lane < count, cell_row >> 7, -1)


def bins_of_step(step, bins, body):
    left = jnp.minimum(STEP_BINS, bins - step * STEP_BINS)
    unroll = 2 if bins % 2 == 0 else 1

    def pair(i, carry):
        for k in range(unroll):
            body(i * unroll + k)
        return carry

    lax.fori_loop(0, left // unroll, pair, 0)


def splat_kernel(
    bins, slots_of, owner, tile, count, cell, offset, velocity, affine, mass, out
):
    step = pl.program_id(0)

    def one(j):
        b = step * STEP_BINS + j
        points = cell.shape[1]
        cells = cell[pl.ds(j, 1), :]
        m = mass[pl.ds(j, 1), :]
        moved = []
        for a in range(3):
            drift = affine[j, pl.ds(3 * a, 1), :] * offset[j, pl.ds(0, 1), :]
            for e in (1, 2):
                drift = drift + affine[j, pl.ds(3 * a + e, 1), :] * offset[j, pl.ds(e, 1), :]
            moved.append(m * (velocity[j, pl.ds(a, 1), :] - drift))
        upper = upper_row(cells, count[b])
        sub = lax.broadcasted_iota(jnp.int32, (8, points), 0)
        hit = (sub & 3) == upper
        first = sub < 4
        halves = []
        for low, high in ((m, moved[0]), (moved[1], moved[2])):
            both = jnp.where(first, low, high)
            halves.append(jnp.where(hit, both, 0.0))
        weighted = jnp.concatenate(halves, axis=0).astype(jnp.bfloat16)
        summed = lax.dot_general(
            weighted,
            lower_hot(cells),
            (((1,), (1,)), ((), ())),
            preferred_element_type=jnp.float32,
        )
        base = pl.multiple_of(j * BLOCK, 8)
        out[pl.ds(base, QROWS), :] = summed
        slot = lax.rem(owner[tile[b]], slots_of).astype(jnp.float32)
        out[pl.ds(base + QROWS, 8), :] = jnp.full((8, LANES), slot, jnp.float32)

    bins_of_step(step, bins, one)


def sample_kernel(bins, slots_of, owner, tile, count, cell, table, out):
    step = pl.program_id(0)

    def one(j):
        b = step * STEP_BINS + j
        points = cell.shape[1]
        cells = cell[pl.ds(j, 1), :]
        slot = lax.rem(owner[tile[b]], slots_of)
        place = jnp.where(b < SELF_BINS, slot, slots_of + b - SELF_BINS)
        rows = table[pl.ds(pl.multiple_of(place * QROWS, 8), QROWS), :].astype(jnp.bfloat16)
        planes = lax.dot_general(
            rows, lower_hot(cells), (((1,), (0,)), ((), ())), preferred_element_type=jnp.float32
        )
        upper = upper_row(cells, count[b])
        half = lax.broadcasted_iota(jnp.int32, (8, points), 0) >> 2
        val = jnp.where(upper == half, planes[0:8], 0.0)
        for k in range(1, GROUPS // 2):
            val = val + jnp.where(upper == half + 2 * k, planes[8 * k : 8 * k + 8], 0.0)
        out[j] = val[0:3] + val[4:7]

    bins_of_step(step, bins, one)


def split(x):
    high = x.astype(jnp.bfloat16)
    low = (x - high.astype(jnp.float32)).astype(jnp.bfloat16)
    return high, low


def pick(hot, x):
    high, low = split(x)
    return jnp.dot(hot, high, preferred_element_type=jnp.float32) + jnp.dot(
        hot, low, preferred_element_type=jnp.float32
    )


def shifted(field, ghost, facing):
    lane = lax.broadcasted_iota(jnp.int32, field.shape, 1)
    stride = (TILE * TILE, TILE, 1)[facing // 2]
    pos = (lane // stride) % TILE
    wrap = stride * (TILE - 1)
    if facing % 2 == 0:
        inner = pltpu.roll(field, CELLS - stride, 1)
        outer = pltpu.roll(ghost, wrap, 1)
        return jnp.where(pos == TILE - 1, outer, inner)
    inner = pltpu.roll(field, stride, 1)
    outer = pltpu.roll(ghost, CELLS - wrap, 1)
    return jnp.where(pos == 0, outer, inner)


def grid_kernel(
    sizes,
    tpd,
    per,
    near_pad,
    lin_row,
    lin_col,
    parts,
    out_vel,
    out_p,
    out_table,
    lins,
    got,
    vel_t,
    p_t,
    reply,
    back,
    part_send,
    part_recv,
    lin_send,
    lin_recv,
    face_send,
    face_recv,
    reply_send,
    reply_recv,
):
    me = [lax.axis_index(name) for name in AXES]

    def inside(rel):
        ok = None
        for n in range(3):
            if rel[n] == 0:
                continue
            one = me[n] < sizes[n] - 1 if rel[n] > 0 else me[n] > 0
            ok = one if ok is None else jnp.logical_and(ok, one)
        return ok

    def at(rel):
        return tuple(
            jnp.clip(me[n] + rel[n], 0, sizes[n] - 1) if rel[n] else me[n] for n in range(3)
        )

    def neg(rel):
        return tuple(-v for v in rel)

    lins[...] = jnp.full(lins.shape, -1, jnp.int32)
    got[...] = jnp.zeros(got.shape, jnp.float32)
    vel_t[...] = jnp.zeros(vel_t.shape, jnp.float32)
    p_t[...] = jnp.zeros(p_t.shape, jnp.float32)
    back[...] = jnp.zeros(back.shape, jnp.float32)

    barrier = pltpu.get_barrier_semaphore()
    for rel in OFFSETS:

        @pl.when(inside(rel))
        def _(rel=rel):
            pl.semaphore_signal(barrier, inc=1, device_id=at(rel), device_id_type=MESH)

    spans = [
        1 + (me[n] > 0).astype(jnp.int32) + (me[n] < sizes[n] - 1).astype(jnp.int32)
        for n in range(3)
    ]
    pl.semaphore_wait(barrier, spans[0] * spans[1] * spans[2] - 1)

    def part_copy(number):
        rows = per * BLOCK
        return pltpu.make_async_remote_copy(
            src_ref=parts.at[pl.ds(SELF_BINS * BLOCK + number * rows, rows)],
            dst_ref=got.at[pl.ds(number * rows, rows)],
            send_sem=part_send.at[number],
            recv_sem=part_recv.at[number],
            device_id=at(OFFSETS[number]),
            device_id_type=MESH,
        )

    def reply_copy(number):
        rows = per * QROWS
        return pltpu.make_async_remote_copy(
            src_ref=reply.at[pl.ds(number * rows, rows)],
            dst_ref=back.at[pl.ds(number * rows, rows)],
            send_sem=reply_send.at[number],
            recv_sem=reply_recv.at[number],
            device_id=at(neg(OFFSETS[number])),
            device_id_type=MESH,
        )

    def lin_copy(d, slot):
        return pltpu.make_async_remote_copy(
            src_ref=lin_row,
            dst_ref=lins.at[slot],
            send_sem=lin_send.at[d],
            recv_sem=lin_recv.at[slot],
            device_id=at(FACES[d]),
            device_id_type=MESH,
        )

    def vel_copy(d, slot):
        return pltpu.make_async_remote_copy(
            src_ref=vel_t.at[:, pl.ds(0, tpd)],
            dst_ref=vel_t.at[:, pl.ds((1 + slot) * tpd, tpd)],
            send_sem=face_send.at[SWEEPS, d],
            recv_sem=face_recv.at[SWEEPS, slot],
            device_id=at(FACES[d]),
            device_id_type=MESH,
        )

    def p_copy(s):
        def make(d, slot):
            return pltpu.make_async_remote_copy(
                src_ref=p_t.at[s, pl.ds(0, tpd)],
                dst_ref=p_t.at[s, pl.ds((1 + slot) * tpd, tpd)],
                send_sem=face_send.at[s, d],
                recv_sem=face_recv.at[s, slot],
                device_id=at(FACES[d]),
                device_id_type=MESH,
            )

        return make

    def start_faces(make):
        for d in range(6):

            @pl.when(inside(FACES[d]))
            def _(d=d):
                make(d, d ^ 1).start()

    def recv_faces(make):
        for d in range(6):

            @pl.when(inside(FACES[d]))
            def _(d=d):
                make(d, d).wait_recv()

    def sent_faces(make):
        for d in range(6):

            @pl.when(inside(FACES[d]))
            def _(d=d):
                make(d, d ^ 1).wait_send()

    for number, rel in enumerate(OFFSETS):

        @pl.when(inside(rel))
        def _(number=number):
            part_copy(number).start()

    start_faces(lin_copy)

    def hot_of(ref, rows):
        slots = ref[pl.ds(QROWS, rows, stride=BLOCK), :]
        lane = lax.broadcasted_iota(jnp.int32, (rows, LANES), 1).astype(jnp.float32)
        return jnp.where(slots == lane, 1.0, 0.0)

    own_hot = jnp.transpose(hot_of(parts, SELF_BINS))[0:tpd].astype(jnp.bfloat16)
    own = [
        pick(own_hot, parts[pl.ds(r, SELF_BINS, stride=BLOCK), :]) for r in range(QROWS)
    ]
    for number, rel in enumerate(OFFSETS):

        @pl.when(inside(neg(rel)))
        def _(number=number):
            part_copy(number).wait_recv()

    near_hot_t = hot_of(got, near_pad)
    near_hot = jnp.transpose(near_hot_t)[0:tpd].astype(jnp.bfloat16)
    pieces = [
        own[r] + pick(near_hot, got[pl.ds(r, near_pad, stride=BLOCK), :]) for r in range(QROWS)
    ]
    totals = [
        jnp.concatenate(pieces[q * GROUPS : (q + 1) * GROUPS], axis=1) for q in range(4)
    ]
    fluid = totals[0] > 0.0
    safe = jnp.where(fluid, totals[0], 1.0)
    vel = [jnp.where(fluid, totals[1 + a] / safe, 0.0) for a in range(3)]
    vel[1] = vel[1] - GRAVITY * jnp.where(fluid, 1.0, 0.0)
    for a in range(3):
        vel_t[a, 0:tpd, :] = vel[a]
    start_faces(vel_copy)

    recv_faces(lin_copy)
    lane = lax.broadcasted_iota(jnp.int32, (8, LANES), 1) // tpd
    cand = jnp.where(lane == 0, lin_row[...], -1)
    for d in range(6):
        cand = jnp.where(lane == d + 1, lins[d], cand)
    here = lin_col[...]
    hots = []
    for face in FACES:
        delta = (face[0] * 1024 + face[1]) * 1024 + face[2]
        hots.append(jnp.where(cand[0:1] == here + delta, 1.0, 0.0))

    recv_faces(vel_copy)
    div = None
    for a in range(3):
        hot = jnp.concatenate(hots[2 * a : 2 * a + 2], axis=0).astype(jnp.bfloat16)
        ghost = pick(hot, vel_t[a])
        term = 0.5 * (
            shifted(vel[a], ghost[0:tpd], 2 * a) - shifted(vel[a], ghost[tpd:], 2 * a + 1)
        )
        div = term if div is None else div + term

    all_hot = jnp.concatenate(hots, axis=0).astype(jnp.bfloat16)
    press = jnp.where(fluid, (0.0 - div) / 6.0, 0.0)
    for s in range(SWEEPS):
        p_t[s, 0:tpd, :] = press
        start_faces(p_copy(s))
        recv_faces(p_copy(s))
        ghost = pick(all_hot, p_t[s])
        sides = [
            shifted(press, ghost[d * tpd : (d + 1) * tpd], d) for d in range(6)
        ]
        if s < SWEEPS - 1:
            total = sides[0]
            for d in range(1, 6):
                total = total + sides[d]
            press = jnp.where(fluid, (total - div) / 6.0, 0.0)
    out_p[...] = press
    near_rows = near_hot_t[:, 0:tpd].astype(jnp.bfloat16)
    for a in range(3):
        v = jnp.where(fluid, vel[a] - 0.5 * (sides[2 * a] - sides[2 * a + 1]), 0.0)
        vel[a] = v
        answer = jnp.dot(near_rows, v.astype(jnp.bfloat16), preferred_element_type=jnp.float32)
        for u in range(GROUPS):
            r = 4 * u + a
            reply[pl.ds(r, near_pad, stride=QROWS), :] = answer[:, u * LANES : (u + 1) * LANES]
    for u in range(GROUPS):
        reply[pl.ds(4 * u + 3, near_pad, stride=QROWS), :] = jnp.zeros(
            (near_pad, LANES), jnp.float32
        )
    for number, rel in enumerate(OFFSETS):

        @pl.when(inside(neg(rel)))
        def _(number=number):
            reply_copy(number).start()

    for a in range(3):
        out_vel[a] = vel[a]
        for u in range(GROUPS):
            out_table[pl.ds(4 * u + a, tpd, stride=QROWS), :] = vel[a][
                :, u * LANES : (u + 1) * LANES
            ]
    for u in range(GROUPS):
        out_table[pl.ds(4 * u + 3, tpd, stride=QROWS), :] = jnp.zeros((tpd, LANES), jnp.float32)

    for number, rel in enumerate(OFFSETS):

        @pl.when(inside(rel))
        def _(number=number):
            part_copy(number).wait_send()

    sent_faces(lin_copy)
    sent_faces(vel_copy)
    for s in range(SWEEPS):
        sent_faces(p_copy(s))
    for number, rel in enumerate(OFFSETS):

        @pl.when(inside(rel))
        def _(number=number):
            reply_copy(number).wait_recv()

        @pl.when(inside(neg(rel)))
        def _(number=number):
            reply_copy(number).wait_send()

    near_rows_all = len(OFFSETS) * per * QROWS
    out_table[pl.ds(tpd * QROWS, near_rows_all), :] = back[...]


def local(
    sizes,
    tile_coords,
    owner_map,
    bin_tile,
    bin_count,
    part_cell,
    part_offset,
    part_velocity,
    part_affine,
    part_mass,
):
    tpd = tile_coords.shape[1]
    bins, points = part_cell.shape
    near = bins - SELF_BINS
    per = near // len(OFFSETS)
    near_pad = -(-near // 8) * 8
    steps = -(-bins // STEP_BINS)
    f32 = jnp.float32

    def rows(i, *_):
        return (i, 0)

    def slabs(i, *_):
        return (i, 0, 0)

    parts = pl.pallas_call(
        functools.partial(splat_kernel, bins, tpd),
        out_shape=jax.ShapeDtypeStruct((bins * BLOCK, LANES), f32),
        grid_spec=pltpu.PrefetchScalarGridSpec(
            num_scalar_prefetch=3,
            grid=(steps,),
            in_specs=[
                pl.BlockSpec((STEP_BINS, points), rows),
                pl.BlockSpec((STEP_BINS, 3, points), slabs),
                pl.BlockSpec((STEP_BINS, 3, points), slabs),
                pl.BlockSpec((STEP_BINS, 9, points), slabs),
                pl.BlockSpec((STEP_BINS, points), rows),
            ],
            out_specs=pl.BlockSpec((STEP_BINS * BLOCK, LANES), rows),
        ),
        compiler_params=pltpu.CompilerParams(dimension_semantics=("arbitrary",)),
        name="splat",
    )(owner_map, bin_tile, bin_count, part_cell, part_offset, part_velocity, part_affine, part_mass)

    lin = (tile_coords[0] * 1024 + tile_coords[1]) * 1024 + tile_coords[2]
    lin_row = jnp.broadcast_to(jnp.tile(lin, LANES // tpd)[None, :], (8, LANES))
    lin_col = jnp.broadcast_to(lin[:, None], (tpd, LANES))
    vmem = pl.BlockSpec(memory_space=pltpu.VMEM)
    dma = pltpu.SemaphoreType.DMA
    count = len(OFFSETS)
    velocity, pressure, table = pl.pallas_call(
        functools.partial(grid_kernel, sizes, tpd, per, near_pad),
        out_shape=(
            jax.ShapeDtypeStruct((3, tpd, CELLS), f32),
            jax.ShapeDtypeStruct((tpd, CELLS), f32),
            jax.ShapeDtypeStruct(((tpd + near) * QROWS, LANES), f32),
        ),
        in_specs=[vmem] * 3,
        out_specs=(vmem, vmem, vmem),
        scratch_shapes=[
            pltpu.VMEM((6, 8, LANES), jnp.int32),
            pltpu.VMEM((near_pad * BLOCK, LANES), f32),
            pltpu.VMEM((3, LANES, CELLS), f32),
            pltpu.VMEM((SWEEPS, LANES, CELLS), f32),
            pltpu.VMEM((near_pad * QROWS, LANES), f32),
            pltpu.VMEM((near * QROWS, LANES), f32),
            dma((count,)),
            dma((count,)),
            dma((6,)),
            dma((6,)),
            dma((SWEEPS + 1, 6)),
            dma((SWEEPS + 1, 6)),
            dma((count,)),
            dma((count,)),
        ],
        compiler_params=pltpu.CompilerParams(collective_id=0, has_side_effects=True),
        name="grid",
    )(lin_row, lin_col, parts)

    sampled = pl.pallas_call(
        functools.partial(sample_kernel, bins, tpd),
        out_shape=jax.ShapeDtypeStruct((bins, 3, points), f32),
        grid_spec=pltpu.PrefetchScalarGridSpec(
            num_scalar_prefetch=3,
            grid=(steps,),
            in_specs=[
                pl.BlockSpec((STEP_BINS, points), rows),
                pl.BlockSpec(((tpd + near) * QROWS, LANES), lambda i, *_: (0, 0)),
            ],
            out_specs=pl.BlockSpec((STEP_BINS, 3, points), slabs),
        ),
        compiler_params=pltpu.CompilerParams(dimension_semantics=("arbitrary",)),
        name="sample",
    )(owner_map, bin_tile, bin_count, part_cell, table)
    return velocity.reshape(3, tpd * CELLS), pressure.reshape(-1), sampled


def solution(mesh):
    split_all = AXES
    placed = (
        P(None, split_all),
        P(),
        P(split_all),
        P(split_all),
        P(split_all, None),
        P(split_all, None, None),
        P(split_all, None, None),
        P(split_all, None, None),
        P(split_all, None),
    )
    sizes = tuple(mesh.shape[name] for name in AXES)
    return jax.shard_map(
        functools.partial(local, sizes),
        mesh=mesh,
        in_specs=placed,
        out_specs=(P(None, split_all), P(split_all), P(split_all, None, None)),
        check_vma=False,
    )
```

```python
import functools

import jax
import jax.numpy as jnp
from jax import lax
from jax.experimental import pallas as pl
from jax.experimental.pallas import tpu as pltpu
from jax.sharding import PartitionSpec as P

TILE = 8
SELF_BINS = 32
SWEEPS = 4
CELLS = TILE * TILE * TILE
LANES = 128
GROUPS = CELLS // LANES
QROWS = 4 * GROUPS
BLOCK = QROWS + 8
STEP_BINS = 8
GRAVITY = 0.5
AXES = ("gx", "gy", "gz")
MESH = pl.DeviceIdType.MESH

OFFSETS = [
    (x, y, z)
    for x in (-1, 0, 1)
    for y in (-1, 0, 1)
    for z in (-1, 0, 1)
    if (x, y, z) != (0, 0, 0)
]
FACES = [(1, 0, 0), (-1, 0, 0), (0, 1, 0), (0, -1, 0), (0, 0, 1), (0, 0, -1)]


def lower_hot(cell_row):
    points = cell_row.shape[1]
    low = (cell_row & (LANES - 1)).astype(jnp.float32).astype(jnp.bfloat16)
    rows = lax.broadcasted_iota(jnp.int32, (LANES, points), 0)
    rows = rows.astype(jnp.float32).astype(jnp.bfloat16)
    return jnp.where(rows == low, jnp.bfloat16(1), jnp.bfloat16(0))


def upper_row(cell_row, count):
    lane = lax.broadcasted_iota(jnp.int32, cell_row.shape, 1)
    return jnp.where(lane < count, cell_row >> 7, -1)


def bins_of_step(step, bins, body):
    left = jnp.minimum(STEP_BINS, bins - step * STEP_BINS)
    unroll = 2 if bins % 2 == 0 else 1

    def pair(i, carry):
        for k in range(unroll):
            body(i * unroll + k)
        return carry

    lax.fori_loop(0, left // unroll, pair, 0)


def splat_kernel(
    bins, slots_of, owner, tile, count, cell, offset, velocity, affine, mass, out, dep
):
    step = pl.program_id(0)
    points = cell.shape[1]
    m = mass[...]
    dep[0] = m
    for a in range(3):
        drift = affine[3 * a] * offset[0]
        for e in (1, 2):
            drift = drift + affine[3 * a + e] * offset[e]
        dep[a + 1] = m * (velocity[a] - drift)

    def one(j):
        b = step * STEP_BINS + j
        cells = cell[pl.ds(j, 1), :]
        upper = upper_row(cells, count[b])
        sub = lax.broadcasted_iota(jnp.int32, (8, points), 0)
        hit = (sub & 3) == upper
        first = sub < 4
        halves = []
        for q in (0, 2):
            both = jnp.where(first, dep[q, pl.ds(j, 1), :], dep[q + 1, pl.ds(j, 1), :])
            halves.append(jnp.where(hit, both, 0.0))
        weighted = jnp.concatenate(halves, axis=0).astype(jnp.bfloat16)
        summed = lax.dot_general(
            weighted,
            lower_hot(cells),
            (((1,), (1,)), ((), ())),
            preferred_element_type=jnp.float32,
        )
        base = pl.multiple_of(j * BLOCK, 8)
        out[pl.ds(base, QROWS), :] = summed
        slot = lax.rem(owner[tile[b]], slots_of).astype(jnp.float32)
        out[pl.ds(base + QROWS, 8), :] = jnp.full((8, LANES), slot, jnp.float32)

    bins_of_step(step, bins, one)


def sample_kernel(bins, slots_of, owner, tile, count, cell, table, out):
    step = pl.program_id(0)

    def one(j):
        b = step * STEP_BINS + j
        points = cell.shape[1]
        cells = cell[pl.ds(j, 1), :]
        slot = lax.rem(owner[tile[b]], slots_of)
        place = jnp.where(b < SELF_BINS, slot, slots_of + b - SELF_BINS)
        rows = table[pl.ds(pl.multiple_of(place * QROWS, 8), QROWS), :].astype(jnp.bfloat16)
        planes = lax.dot_general(
            rows, lower_hot(cells), (((1,), (0,)), ((), ())), preferred_element_type=jnp.float32
        )
        upper = upper_row(cells, count[b])
        half = lax.broadcasted_iota(jnp.int32, (8, points), 0) >> 2
        val = jnp.where(upper == half, planes[0:8], 0.0)
        for k in range(1, GROUPS // 2):
            val = val + jnp.where(upper == half + 2 * k, planes[8 * k : 8 * k + 8], 0.0)
        val = val[0:4] + val[4:8]
        for a in range(3):
            out[a, pl.ds(j, 1), :] = val[a : a + 1]

    bins_of_step(step, bins, one)


def split(x):
    high = x.astype(jnp.bfloat16)
    low = (x - high.astype(jnp.float32)).astype(jnp.bfloat16)
    return high, low


def pick(hot, x):
    high, low = split(x)
    return jnp.dot(hot, high, preferred_element_type=jnp.float32) + jnp.dot(
        hot, low, preferred_element_type=jnp.float32
    )


def shifted(field, ghost, facing):
    lane = lax.broadcasted_iota(jnp.int32, field.shape, 1)
    stride = (TILE * TILE, TILE, 1)[facing // 2]
    pos = (lane // stride) % TILE
    wrap = stride * (TILE - 1)
    if facing % 2 == 0:
        inner = pltpu.roll(field, CELLS - stride, 1)
        outer = pltpu.roll(ghost, wrap, 1)
        return jnp.where(pos == TILE - 1, outer, inner)
    inner = pltpu.roll(field, stride, 1)
    outer = pltpu.roll(ghost, CELLS - wrap, 1)
    return jnp.where(pos == 0, outer, inner)


def grid_kernel(
    sizes,
    tpd,
    per,
    near_pad,
    coords,
    parts,
    out_vel,
    out_p,
    out_table,
    lin_row,
    lins,
    got,
    vel_t,
    p_t,
    reply,
    back,
    part_send,
    part_recv,
    lin_send,
    lin_recv,
    face_send,
    face_recv,
    reply_send,
    reply_recv,
):
    me = [lax.axis_index(name) for name in AXES]

    def inside(rel):
        ok = None
        for n in range(3):
            if rel[n] == 0:
                continue
            one = me[n] < sizes[n] - 1 if rel[n] > 0 else me[n] > 0
            ok = one if ok is None else jnp.logical_and(ok, one)
        return ok

    def at(rel):
        return tuple(
            jnp.clip(me[n] + rel[n], 0, sizes[n] - 1) if rel[n] else me[n] for n in range(3)
        )

    def neg(rel):
        return tuple(-v for v in rel)

    lin = (coords[0:1] * 64 + coords[1:2]) * 64 + coords[2:3]
    lin = jnp.concatenate([lin.astype(jnp.float32)] * (LANES // tpd), axis=1)
    lin_row[...] = jnp.broadcast_to(lin, (8, LANES))
    here = jnp.transpose(jnp.broadcast_to(lin, (LANES, LANES)))[0:tpd]
    lins[...] = jnp.full(lins.shape, -1.0, jnp.float32)
    got[...] = jnp.zeros(got.shape, jnp.float32)
    vel_t[...] = jnp.zeros(vel_t.shape, jnp.float32)
    p_t[...] = jnp.zeros(p_t.shape, jnp.float32)
    back[...] = jnp.zeros(back.shape, jnp.float32)

    barrier = pltpu.get_barrier_semaphore()
    for rel in OFFSETS:

        @pl.when(inside(rel))
        def _(rel=rel):
            pl.semaphore_signal(barrier, inc=1, device_id=at(rel), device_id_type=MESH)

    spans = [
        1 + (me[n] > 0).astype(jnp.int32) + (me[n] < sizes[n] - 1).astype(jnp.int32)
        for n in range(3)
    ]
    pl.semaphore_wait(barrier, spans[0] * spans[1] * spans[2] - 1)

    def part_copy(number):
        rows = per * BLOCK
        return pltpu.make_async_remote_copy(
            src_ref=parts.at[pl.ds(SELF_BINS * BLOCK + number * rows, rows)],
            dst_ref=got.at[pl.ds(number * rows, rows)],
            send_sem=part_send.at[number],
            recv_sem=part_recv.at[number],
            device_id=at(OFFSETS[number]),
            device_id_type=MESH,
        )

    def reply_copy(number):
        rows = per * QROWS
        return pltpu.make_async_remote_copy(
            src_ref=reply.at[pl.ds(number * rows, rows)],
            dst_ref=back.at[pl.ds(number * rows, rows)],
            send_sem=reply_send.at[number],
            recv_sem=reply_recv.at[number],
            device_id=at(neg(OFFSETS[number])),
            device_id_type=MESH,
        )

    def lin_copy(d, slot):
        return pltpu.make_async_remote_copy(
            src_ref=lin_row,
            dst_ref=lins.at[slot],
            send_sem=lin_send.at[d],
            recv_sem=lin_recv.at[slot],
            device_id=at(FACES[d]),
            device_id_type=MESH,
        )

    def vel_copy(d, slot):
        return pltpu.make_async_remote_copy(
            src_ref=vel_t.at[:, pl.ds(0, tpd)],
            dst_ref=vel_t.at[:, pl.ds((1 + slot) * tpd, tpd)],
            send_sem=face_send.at[SWEEPS, d],
            recv_sem=face_recv.at[SWEEPS, slot],
            device_id=at(FACES[d]),
            device_id_type=MESH,
        )

    def p_copy(s):
        def make(d, slot):
            return pltpu.make_async_remote_copy(
                src_ref=p_t.at[s, pl.ds(0, tpd)],
                dst_ref=p_t.at[s, pl.ds((1 + slot) * tpd, tpd)],
                send_sem=face_send.at[s, d],
                recv_sem=face_recv.at[s, slot],
                device_id=at(FACES[d]),
                device_id_type=MESH,
            )

        return make

    def start_faces(make):
        for d in range(6):

            @pl.when(inside(FACES[d]))
            def _(d=d):
                make(d, d ^ 1).start()

    def recv_faces(make):
        for d in range(6):

            @pl.when(inside(FACES[d]))
            def _(d=d):
                make(d, d).wait_recv()

    def sent_faces(make):
        for d in range(6):

            @pl.when(inside(FACES[d]))
            def _(d=d):
                make(d, d ^ 1).wait_send()

    for number, rel in enumerate(OFFSETS):

        @pl.when(inside(rel))
        def _(number=number):
            part_copy(number).start()

    start_faces(lin_copy)

    def hot_of(ref, rows):
        slots = ref[pl.ds(QROWS, rows, stride=BLOCK), :]
        lane = lax.broadcasted_iota(jnp.int32, (rows, LANES), 1).astype(jnp.float32)
        return jnp.where(slots == lane, 1.0, 0.0)

    own_hot = jnp.transpose(hot_of(parts, SELF_BINS))[0:tpd].astype(jnp.bfloat16)
    own = [
        pick(own_hot, parts[pl.ds(r, SELF_BINS, stride=BLOCK), :]) for r in range(QROWS)
    ]
    for number, rel in enumerate(OFFSETS):

        @pl.when(inside(neg(rel)))
        def _(number=number):
            part_copy(number).wait_recv()

    near_hot_t = hot_of(got, near_pad)
    near_hot = jnp.transpose(near_hot_t)[0:tpd].astype(jnp.bfloat16)
    pieces = [
        own[r] + pick(near_hot, got[pl.ds(r, near_pad, stride=BLOCK), :]) for r in range(QROWS)
    ]
    totals = [
        jnp.concatenate(pieces[q * GROUPS : (q + 1) * GROUPS], axis=1) for q in range(4)
    ]
    fluid = totals[0] > 0.0
    safe = jnp.where(fluid, totals[0], 1.0)
    vel = [jnp.where(fluid, totals[1 + a] / safe, 0.0) for a in range(3)]
    vel[1] = vel[1] - GRAVITY * jnp.where(fluid, 1.0, 0.0)
    for a in range(3):
        vel_t[a, 0:tpd, :] = vel[a]
    start_faces(vel_copy)

    recv_faces(lin_copy)
    lane = lax.broadcasted_iota(jnp.int32, (8, LANES), 1) // tpd
    cand = jnp.where(lane == 0, lin_row[...], -1.0)
    for d in range(6):
        cand = jnp.where(lane == d + 1, lins[d], cand)
    hots = []
    for face in FACES:
        delta = float((face[0] * 64 + face[1]) * 64 + face[2])
        hots.append(jnp.where(cand[0:1] == here + delta, 1.0, 0.0))

    recv_faces(vel_copy)
    div = None
    for a in range(3):
        hot = jnp.concatenate(hots[2 * a : 2 * a + 2], axis=0).astype(jnp.bfloat16)
        ghost = pick(hot, vel_t[a])
        term = 0.5 * (
            shifted(vel[a], ghost[0:tpd], 2 * a) - shifted(vel[a], ghost[tpd:], 2 * a + 1)
        )
        div = term if div is None else div + term

    all_hot = jnp.concatenate(hots, axis=0).astype(jnp.bfloat16)
    press = jnp.where(fluid, (0.0 - div) / 6.0, 0.0)
    for s in range(SWEEPS):
        p_t[s, 0:tpd, :] = press
        start_faces(p_copy(s))
        recv_faces(p_copy(s))
        ghost = pick(all_hot, p_t[s])
        sides = [
            shifted(press, ghost[d * tpd : (d + 1) * tpd], d) for d in range(6)
        ]
        if s < SWEEPS - 1:
            total = sides[0]
            for d in range(1, 6):
                total = total + sides[d]
            press = jnp.where(fluid, (total - div) / 6.0, 0.0)
    for u in range(GROUPS):
        out_p[pl.ds(u, tpd, stride=GROUPS), :] = press[:, u * LANES : (u + 1) * LANES]
    near_rows = near_hot_t[:, 0:tpd].astype(jnp.bfloat16)
    for a in range(3):
        v = jnp.where(fluid, vel[a] - 0.5 * (sides[2 * a] - sides[2 * a + 1]), 0.0)
        vel[a] = v
        answer = jnp.dot(near_rows, v.astype(jnp.bfloat16), preferred_element_type=jnp.float32)
        for u in range(GROUPS):
            r = 4 * u + a
            reply[pl.ds(r, near_pad, stride=QROWS), :] = answer[:, u * LANES : (u + 1) * LANES]
    for u in range(GROUPS):
        reply[pl.ds(4 * u + 3, near_pad, stride=QROWS), :] = jnp.zeros(
            (near_pad, LANES), jnp.float32
        )
    for number, rel in enumerate(OFFSETS):

        @pl.when(inside(neg(rel)))
        def _(number=number):
            reply_copy(number).start()

    for a in range(3):
        for t in range(tpd):
            out_vel[a : a + 1, t * CELLS : (t + 1) * CELLS] = vel[a][t : t + 1]
        for u in range(GROUPS):
            out_table[pl.ds(4 * u + a, tpd, stride=QROWS), :] = vel[a][
                :, u * LANES : (u + 1) * LANES
            ]
    for u in range(GROUPS):
        out_table[pl.ds(4 * u + 3, tpd, stride=QROWS), :] = jnp.zeros((tpd, LANES), jnp.float32)

    for number, rel in enumerate(OFFSETS):

        @pl.when(inside(rel))
        def _(number=number):
            part_copy(number).wait_send()

    sent_faces(lin_copy)
    sent_faces(vel_copy)
    for s in range(SWEEPS):
        sent_faces(p_copy(s))
    for number, rel in enumerate(OFFSETS):

        @pl.when(inside(rel))
        def _(number=number):
            reply_copy(number).wait_recv()

        @pl.when(inside(neg(rel)))
        def _(number=number):
            reply_copy(number).wait_send()

    near_rows_all = len(OFFSETS) * per * QROWS
    out_table[pl.ds(tpd * QROWS, near_rows_all), :] = back[...]


def local(
    sizes,
    tile_coords,
    owner_map,
    bin_tile,
    bin_count,
    part_cell,
    part_offset,
    part_velocity,
    part_affine,
    part_mass,
):
    tpd = tile_coords.shape[1]
    bins, points = part_cell.shape
    near = bins - SELF_BINS
    per = near // len(OFFSETS)
    near_pad = -(-near // 8) * 8
    steps = -(-bins // STEP_BINS)
    f32 = jnp.float32

    def rows(i, *_):
        return (i, 0)

    def slabs(i, *_):
        return (0, i, 0)

    by_component = [
        jnp.transpose(x, (1, 0, 2)) for x in (part_offset, part_velocity, part_affine)
    ]
    parts = pl.pallas_call(
        functools.partial(splat_kernel, bins, tpd),
        out_shape=jax.ShapeDtypeStruct((bins * BLOCK, LANES), f32),
        grid_spec=pltpu.PrefetchScalarGridSpec(
            num_scalar_prefetch=3,
            grid=(steps,),
            in_specs=[
                pl.BlockSpec((STEP_BINS, points), rows),
                pl.BlockSpec((3, STEP_BINS, points), slabs),
                pl.BlockSpec((3, STEP_BINS, points), slabs),
                pl.BlockSpec((9, STEP_BINS, points), slabs),
                pl.BlockSpec((STEP_BINS, points), rows),
            ],
            out_specs=pl.BlockSpec((STEP_BINS * BLOCK, LANES), rows),
            scratch_shapes=[pltpu.VMEM((4, STEP_BINS, points), f32)],
        ),
        compiler_params=pltpu.CompilerParams(dimension_semantics=("arbitrary",)),
        name="splat",
    )(owner_map, bin_tile, bin_count, part_cell, *by_component, part_mass)

    vmem = pl.BlockSpec(memory_space=pltpu.VMEM)
    dma = pltpu.SemaphoreType.DMA
    count = len(OFFSETS)
    velocity, pressure, table = pl.pallas_call(
        functools.partial(grid_kernel, sizes, tpd, per, near_pad),
        out_shape=(
            jax.ShapeDtypeStruct((3, tpd * CELLS), f32),
            jax.ShapeDtypeStruct((tpd * GROUPS, LANES), f32),
            jax.ShapeDtypeStruct(((tpd + near) * QROWS, LANES), f32),
        ),
        in_specs=[vmem] * 2,
        out_specs=(vmem, vmem, vmem),
        scratch_shapes=[
            pltpu.VMEM((8, LANES), f32),
            pltpu.VMEM((6, 8, LANES), f32),
            pltpu.VMEM((near_pad * BLOCK, LANES), f32),
            pltpu.VMEM((3, LANES, CELLS), f32),
            pltpu.VMEM((SWEEPS, LANES, CELLS), f32),
            pltpu.VMEM((near_pad * QROWS, LANES), f32),
            pltpu.VMEM((near * QROWS, LANES), f32),
            dma((count,)),
            dma((count,)),
            dma((6,)),
            dma((6,)),
            dma((SWEEPS + 1, 6)),
            dma((SWEEPS + 1, 6)),
            dma((count,)),
            dma((count,)),
        ],
        compiler_params=pltpu.CompilerParams(collective_id=0, has_side_effects=True),
        name="grid",
    )(tile_coords, parts)

    sampled = pl.pallas_call(
        functools.partial(sample_kernel, bins, tpd),
        out_shape=jax.ShapeDtypeStruct((3, bins, points), f32),
        grid_spec=pltpu.PrefetchScalarGridSpec(
            num_scalar_prefetch=3,
            grid=(steps,),
            in_specs=[
                pl.BlockSpec((STEP_BINS, points), rows),
                pl.BlockSpec(((tpd + near) * QROWS, LANES), lambda i, *_: (0, 0)),
            ],
            out_specs=pl.BlockSpec((3, STEP_BINS, points), slabs),
        ),
        compiler_params=pltpu.CompilerParams(dimension_semantics=("arbitrary",)),
        name="sample",
    )(owner_map, bin_tile, bin_count, part_cell, table)
    return velocity, pressure.reshape(-1), jnp.transpose(sampled, (1, 0, 2))


def solution(mesh):
    split_all = AXES
    placed = (
        P(None, split_all),
        P(),
        P(split_all),
        P(split_all),
        P(split_all, None),
        P(split_all, None, None),
        P(split_all, None, None),
        P(split_all, None, None),
        P(split_all, None),
    )
    sizes = tuple(mesh.shape[name] for name in AXES)
    return jax.shard_map(
        functools.partial(local, sizes),
        mesh=mesh,
        in_specs=placed,
        out_specs=(P(None, split_all), P(split_all), P(split_all, None, None)),
        check_vma=False,
    )
```

```python
import functools

import jax
import jax.numpy as jnp
from jax import lax
from jax.experimental import pallas as pl
from jax.experimental.pallas import tpu as pltpu
from jax.sharding import PartitionSpec as P

TILE = 8
SELF_BINS = 32
SWEEPS = 4
CELLS = TILE * TILE * TILE
LANES = 128
GROUPS = CELLS // LANES
QROWS = 4 * GROUPS
BLOCK = QROWS + 8
STEP_BINS = 8
GRAVITY = 0.5
AXES = ("gx", "gy", "gz")
MESH = pl.DeviceIdType.MESH

OFFSETS = [
    (x, y, z)
    for x in (-1, 0, 1)
    for y in (-1, 0, 1)
    for z in (-1, 0, 1)
    if (x, y, z) != (0, 0, 0)
]
FACES = [(1, 0, 0), (-1, 0, 0), (0, 1, 0), (0, -1, 0), (0, 0, 1), (0, 0, -1)]


def lower_hot(cell_row):
    points = cell_row.shape[1]
    low = (cell_row & (LANES - 1)).astype(jnp.float32).astype(jnp.bfloat16)
    rows = lax.broadcasted_iota(jnp.int32, (LANES, points), 0)
    rows = rows.astype(jnp.float32).astype(jnp.bfloat16)
    return jnp.where(rows == low, jnp.bfloat16(1), jnp.bfloat16(0))


def upper_row(cell_row, count):
    lane = lax.broadcasted_iota(jnp.int32, cell_row.shape, 1)
    return jnp.where(lane < count, cell_row >> 7, -1)


def bins_of_step(step, bins, body):
    left = jnp.minimum(STEP_BINS, bins - step * STEP_BINS)
    unroll = 2 if bins % 2 == 0 else 1

    def pair(i, carry):
        for k in range(unroll):
            body(i * unroll + k)
        return carry

    lax.fori_loop(0, left // unroll, pair, 0)


def splat_kernel(
    bins, slots_of, owner, tile, count, cell, offset, velocity, affine, mass, out, dep
):
    step = pl.program_id(0)
    points = cell.shape[1]
    m = mass[...]
    dep[0] = m
    for a in range(3):
        drift = affine[3 * a] * offset[0]
        for e in (1, 2):
            drift = drift + affine[3 * a + e] * offset[e]
        dep[a + 1] = m * (velocity[a] - drift)

    def one(j):
        b = step * STEP_BINS + j
        cells = cell[pl.ds(j, 1), :]
        upper = upper_row(cells, count[b])
        sub = lax.broadcasted_iota(jnp.int32, (8, points), 0)
        hit = (sub & 3) == upper
        first = sub < 4
        halves = []
        for q in (0, 2):
            both = jnp.where(first, dep[q, pl.ds(j, 1), :], dep[q + 1, pl.ds(j, 1), :])
            halves.append(jnp.where(hit, both, 0.0))
        weighted = jnp.concatenate(halves, axis=0).astype(jnp.bfloat16)
        summed = lax.dot_general(
            weighted,
            lower_hot(cells),
            (((1,), (1,)), ((), ())),
            preferred_element_type=jnp.float32,
        )
        base = pl.multiple_of(j * BLOCK, 8)
        out[pl.ds(base, QROWS), :] = summed
        slot = lax.rem(owner[tile[b]], slots_of).astype(jnp.float32)
        out[pl.ds(base + QROWS, 8), :] = jnp.full((8, LANES), slot, jnp.float32)

    bins_of_step(step, bins, one)


def sample_kernel(bins, slots_of, owner, tile, count, cell, table, out):
    step = pl.program_id(0)

    def one(j):
        b = step * STEP_BINS + j
        points = cell.shape[1]
        cells = cell[pl.ds(j, 1), :]
        slot = lax.rem(owner[tile[b]], slots_of)
        place = jnp.where(b < SELF_BINS, slot, slots_of + b - SELF_BINS)
        rows = table[pl.ds(pl.multiple_of(place * QROWS, 8), QROWS), :].astype(jnp.bfloat16)
        planes = lax.dot_general(
            rows, lower_hot(cells), (((1,), (0,)), ((), ())), preferred_element_type=jnp.float32
        )
        upper = upper_row(cells, count[b])
        half = lax.broadcasted_iota(jnp.int32, (8, points), 0) >> 2
        val = jnp.where(upper == half, planes[0:8], 0.0)
        for k in range(1, GROUPS // 2):
            val = val + jnp.where(upper == half + 2 * k, planes[8 * k : 8 * k + 8], 0.0)
        val = val[0:4] + val[4:8]
        for a in range(3):
            out[a, pl.ds(j, 1), :] = val[a : a + 1]

    bins_of_step(step, bins, one)


def split(x):
    high = x.astype(jnp.bfloat16)
    low = (x - high.astype(jnp.float32)).astype(jnp.bfloat16)
    return high, low


def pick(hot, x):
    high, low = split(x)
    return jnp.dot(hot, high, preferred_element_type=jnp.float32) + jnp.dot(
        hot, low, preferred_element_type=jnp.float32
    )


def tile_of(x, u):
    return x[:, u * LANES : (u + 1) * LANES]


def pack_faces(field, axis):
    lane = lax.broadcasted_iota(jnp.int32, (field.shape[0], LANES), 1)
    half = TILE * TILE
    if axis == 0:
        both = jnp.where(lane < half, tile_of(field, 0), tile_of(field, GROUPS - 1))
        return pltpu.roll(both, half, 1)
    stride = (TILE, 1)[axis - 1]
    pos = (lane // stride) % TILE
    packed = jnp.zeros((field.shape[0], LANES), jnp.float32)
    for u in range(GROUPS):
        low = (TILE - 1 - u) * stride
        piece = tile_of(field, u)
        packed = jnp.where(pos == TILE - 1 - u, pltpu.roll(piece, low, 1), packed)
        packed = jnp.where(pos == u, pltpu.roll(piece, LANES - low, 1), packed)
    return packed


def shifted(field, ghost, facing):
    lane = lax.broadcasted_iota(jnp.int32, field.shape, 1)
    stride = (TILE * TILE, TILE, 1)[facing // 2]
    pos = (lane // stride) % TILE
    outer = []
    for u in range(GROUPS):
        move = 0 if facing < 2 else u * stride
        if move and facing % 2:
            move = LANES - move
        outer.append(pltpu.roll(ghost, move, 1) if move else ghost)
    outer = jnp.concatenate(outer, axis=1)
    if facing % 2 == 0:
        return jnp.where(pos == TILE - 1, outer, pltpu.roll(field, CELLS - stride, 1))
    return jnp.where(pos == 0, outer, pltpu.roll(field, stride, 1))


def grid_kernel(
    sizes,
    tpd,
    per,
    near_pad,
    coords,
    parts,
    out_vel,
    out_p,
    out_table,
    lin_row,
    lins,
    got,
    vel_t,
    p_t,
    reply,
    back,
    part_send,
    part_recv,
    lin_send,
    lin_recv,
    face_send,
    face_recv,
    reply_send,
    reply_recv,
):
    me = [lax.axis_index(name) for name in AXES]

    def inside(rel):
        ok = None
        for n in range(3):
            if rel[n] == 0:
                continue
            one = me[n] < sizes[n] - 1 if rel[n] > 0 else me[n] > 0
            ok = one if ok is None else jnp.logical_and(ok, one)
        return ok

    def at(rel):
        return tuple(
            jnp.clip(me[n] + rel[n], 0, sizes[n] - 1) if rel[n] else me[n] for n in range(3)
        )

    def neg(rel):
        return tuple(-v for v in rel)

    lin = (coords[0:1] * 64 + coords[1:2]) * 64 + coords[2:3]
    lin = jnp.concatenate([lin.astype(jnp.float32)] * (LANES // tpd), axis=1)
    lin_row[...] = jnp.broadcast_to(lin, (8, LANES))
    here = jnp.transpose(jnp.broadcast_to(lin, (LANES, LANES)))[0:tpd]
    lins[...] = jnp.full(lins.shape, -1.0, jnp.float32)
    got[...] = jnp.zeros(got.shape, jnp.float32)
    vel_t[...] = jnp.zeros(vel_t.shape, jnp.float32)
    p_t[...] = jnp.zeros(p_t.shape, jnp.float32)
    back[...] = jnp.zeros(back.shape, jnp.float32)

    barrier = pltpu.get_barrier_semaphore()
    for rel in OFFSETS:

        @pl.when(inside(rel))
        def _(rel=rel):
            pl.semaphore_signal(barrier, inc=1, device_id=at(rel), device_id_type=MESH)

    spans = [
        1 + (me[n] > 0).astype(jnp.int32) + (me[n] < sizes[n] - 1).astype(jnp.int32)
        for n in range(3)
    ]
    pl.semaphore_wait(barrier, spans[0] * spans[1] * spans[2] - 1)

    def part_copy(number):
        start = number * per * BLOCK
        rows = (per - 1) * BLOCK + QROWS + 1
        return pltpu.make_async_remote_copy(
            src_ref=parts.at[pl.ds(SELF_BINS * BLOCK + start, rows)],
            dst_ref=got.at[pl.ds(start, rows)],
            send_sem=part_send.at[number],
            recv_sem=part_recv.at[number],
            device_id=at(OFFSETS[number]),
            device_id_type=MESH,
        )

    def reply_copy(number):
        rows = per * QROWS
        return pltpu.make_async_remote_copy(
            src_ref=reply.at[pl.ds(number * rows, rows)],
            dst_ref=back.at[pl.ds(number * rows, rows)],
            send_sem=reply_send.at[number],
            recv_sem=reply_recv.at[number],
            device_id=at(neg(OFFSETS[number])),
            device_id_type=MESH,
        )

    def lin_copy(d, slot):
        return pltpu.make_async_remote_copy(
            src_ref=lin_row,
            dst_ref=lins.at[slot],
            send_sem=lin_send.at[d],
            recv_sem=lin_recv.at[slot],
            device_id=at(FACES[d]),
            device_id_type=MESH,
        )

    def vel_copy(d, slot):
        return pltpu.make_async_remote_copy(
            src_ref=vel_t.at[pl.ds(0, tpd)],
            dst_ref=vel_t.at[pl.ds((1 + slot) * tpd, tpd)],
            send_sem=face_send.at[SWEEPS, d],
            recv_sem=face_recv.at[SWEEPS, slot],
            device_id=at(FACES[d]),
            device_id_type=MESH,
        )

    def p_copy(s):
        def make(d, slot):
            return pltpu.make_async_remote_copy(
                src_ref=p_t.at[s, pl.ds(0, tpd)],
                dst_ref=p_t.at[s, pl.ds((1 + slot) * tpd, tpd)],
                send_sem=face_send.at[s, d],
                recv_sem=face_recv.at[s, slot],
                device_id=at(FACES[d]),
                device_id_type=MESH,
            )

        return make

    def start_faces(make):
        for d in range(6):

            @pl.when(inside(FACES[d]))
            def _(d=d):
                make(d, d ^ 1).start()

    def recv_faces(make):
        for d in range(6):

            @pl.when(inside(FACES[d]))
            def _(d=d):
                make(d, d).wait_recv()

    def sent_faces(make):
        for d in range(6):

            @pl.when(inside(FACES[d]))
            def _(d=d):
                make(d, d ^ 1).wait_send()

    for number, rel in enumerate(OFFSETS):

        @pl.when(inside(rel))
        def _(number=number):
            part_copy(number).start()

    start_faces(lin_copy)

    def hot_of(ref, rows):
        slots = ref[pl.ds(QROWS, rows, stride=BLOCK), :]
        lane = lax.broadcasted_iota(jnp.int32, (rows, LANES), 1).astype(jnp.float32)
        return jnp.where(slots == lane, 1.0, 0.0)

    own_hot = jnp.transpose(hot_of(parts, SELF_BINS))[0:tpd].astype(jnp.bfloat16)
    own = [
        pick(own_hot, parts[pl.ds(r, SELF_BINS, stride=BLOCK), :]) for r in range(QROWS)
    ]
    for number, rel in enumerate(OFFSETS):

        @pl.when(inside(neg(rel)))
        def _(number=number):
            part_copy(number).wait_recv()

    near_hot_t = hot_of(got, near_pad)
    near_hot = jnp.transpose(near_hot_t)[0:tpd].astype(jnp.bfloat16)
    pieces = [
        own[r] + pick(near_hot, got[pl.ds(r, near_pad, stride=BLOCK), :]) for r in range(QROWS)
    ]
    totals = [
        jnp.concatenate(pieces[q * GROUPS : (q + 1) * GROUPS], axis=1) for q in range(4)
    ]
    fluid = totals[0] > 0.0
    safe = jnp.where(fluid, totals[0], 1.0)
    vel = [jnp.where(fluid, totals[1 + a] / safe, 0.0) for a in range(3)]
    vel[1] = vel[1] - GRAVITY * jnp.where(fluid, 1.0, 0.0)
    for a in range(3):
        vel_t[0:tpd, a * LANES : (a + 1) * LANES] = pack_faces(vel[a], a)
    start_faces(vel_copy)

    recv_faces(lin_copy)
    lane = lax.broadcasted_iota(jnp.int32, (8, LANES), 1) // tpd
    cand = jnp.where(lane == 0, lin_row[...], -1.0)
    for d in range(6):
        cand = jnp.where(lane == d + 1, lins[d], cand)
    hots = []
    for face in FACES:
        delta = float((face[0] * 64 + face[1]) * 64 + face[2])
        hots.append(jnp.where(cand[0:1] == here + delta, 1.0, 0.0))

    pair_hots = [
        jnp.concatenate(hots[2 * a : 2 * a + 2], axis=0).astype(jnp.bfloat16) for a in range(3)
    ]
    recv_faces(vel_copy)
    div = None
    for a in range(3):
        ghost = pick(pair_hots[a], vel_t[:, a * LANES : (a + 1) * LANES])
        term = 0.5 * (
            shifted(vel[a], ghost[0:tpd], 2 * a) - shifted(vel[a], ghost[tpd:], 2 * a + 1)
        )
        div = term if div is None else div + term

    press = jnp.where(fluid, (0.0 - div) / 6.0, 0.0)
    for s in range(SWEEPS):
        for a in range(3):
            p_t[s, 0:tpd, a * LANES : (a + 1) * LANES] = pack_faces(press, a)
        start_faces(p_copy(s))
        recv_faces(p_copy(s))
        sides = []
        for a in range(3):
            ghost = pick(pair_hots[a], p_t[s, :, a * LANES : (a + 1) * LANES])
            sides.append(shifted(press, ghost[0:tpd], 2 * a))
            sides.append(shifted(press, ghost[tpd:], 2 * a + 1))
        if s < SWEEPS - 1:
            total = sides[0]
            for d in range(1, 6):
                total = total + sides[d]
            press = jnp.where(fluid, (total - div) / 6.0, 0.0)
    for u in range(GROUPS):
        out_p[pl.ds(u, tpd, stride=GROUPS), :] = press[:, u * LANES : (u + 1) * LANES]
    near_rows = near_hot_t[:, 0:tpd].astype(jnp.bfloat16)
    for a in range(3):
        v = jnp.where(fluid, vel[a] - 0.5 * (sides[2 * a] - sides[2 * a + 1]), 0.0)
        vel[a] = v
        answer = jnp.dot(near_rows, v.astype(jnp.bfloat16), preferred_element_type=jnp.float32)
        for u in range(GROUPS):
            r = 4 * u + a
            reply[pl.ds(r, near_pad, stride=QROWS), :] = answer[:, u * LANES : (u + 1) * LANES]
    for u in range(GROUPS):
        reply[pl.ds(4 * u + 3, near_pad, stride=QROWS), :] = jnp.zeros(
            (near_pad, LANES), jnp.float32
        )
    for number, rel in enumerate(OFFSETS):

        @pl.when(inside(neg(rel)))
        def _(number=number):
            reply_copy(number).start()

    for a in range(3):
        for t in range(tpd):
            out_vel[a : a + 1, t * CELLS : (t + 1) * CELLS] = vel[a][t : t + 1]
        for u in range(GROUPS):
            out_table[pl.ds(4 * u + a, tpd, stride=QROWS), :] = vel[a][
                :, u * LANES : (u + 1) * LANES
            ]
    for u in range(GROUPS):
        out_table[pl.ds(4 * u + 3, tpd, stride=QROWS), :] = jnp.zeros((tpd, LANES), jnp.float32)

    for number, rel in enumerate(OFFSETS):

        @pl.when(inside(rel))
        def _(number=number):
            part_copy(number).wait_send()

    sent_faces(lin_copy)
    sent_faces(vel_copy)
    for s in range(SWEEPS):
        sent_faces(p_copy(s))
    for number, rel in enumerate(OFFSETS):

        @pl.when(inside(rel))
        def _(number=number):
            reply_copy(number).wait_recv()

        @pl.when(inside(neg(rel)))
        def _(number=number):
            reply_copy(number).wait_send()

    near_rows_all = len(OFFSETS) * per * QROWS
    out_table[pl.ds(tpd * QROWS, near_rows_all), :] = back[...]


def local(
    sizes,
    tile_coords,
    owner_map,
    bin_tile,
    bin_count,
    part_cell,
    part_offset,
    part_velocity,
    part_affine,
    part_mass,
):
    tpd = tile_coords.shape[1]
    bins, points = part_cell.shape
    near = bins - SELF_BINS
    per = near // len(OFFSETS)
    near_pad = -(-near // 8) * 8
    steps = -(-bins // STEP_BINS)
    f32 = jnp.float32

    def rows(i, *_):
        return (i, 0)

    def slabs(i, *_):
        return (0, i, 0)

    by_component = [
        jnp.transpose(x, (1, 0, 2)) for x in (part_offset, part_velocity, part_affine)
    ]
    parts = pl.pallas_call(
        functools.partial(splat_kernel, bins, tpd),
        out_shape=jax.ShapeDtypeStruct((bins * BLOCK, LANES), f32),
        grid_spec=pltpu.PrefetchScalarGridSpec(
            num_scalar_prefetch=3,
            grid=(steps,),
            in_specs=[
                pl.BlockSpec((STEP_BINS, points), rows),
                pl.BlockSpec((3, STEP_BINS, points), slabs),
                pl.BlockSpec((3, STEP_BINS, points), slabs),
                pl.BlockSpec((9, STEP_BINS, points), slabs),
                pl.BlockSpec((STEP_BINS, points), rows),
            ],
            out_specs=pl.BlockSpec((STEP_BINS * BLOCK, LANES), rows),
            scratch_shapes=[pltpu.VMEM((4, STEP_BINS, points), f32)],
        ),
        compiler_params=pltpu.CompilerParams(dimension_semantics=("arbitrary",)),
        name="splat",
    )(owner_map, bin_tile, bin_count, part_cell, *by_component, part_mass)

    vmem = pl.BlockSpec(memory_space=pltpu.VMEM)
    dma = pltpu.SemaphoreType.DMA
    count = len(OFFSETS)
    velocity, pressure, table = pl.pallas_call(
        functools.partial(grid_kernel, sizes, tpd, per, near_pad),
        out_shape=(
            jax.ShapeDtypeStruct((3, tpd * CELLS), f32),
            jax.ShapeDtypeStruct((tpd * GROUPS, LANES), f32),
            jax.ShapeDtypeStruct(((tpd + near) * QROWS, LANES), f32),
        ),
        in_specs=[vmem] * 2,
        out_specs=(vmem, vmem, vmem),
        scratch_shapes=[
            pltpu.VMEM((8, LANES), f32),
            pltpu.VMEM((6, 8, LANES), f32),
            pltpu.VMEM((near_pad * BLOCK, LANES), f32),
            pltpu.VMEM((LANES, 3 * LANES), f32),
            pltpu.VMEM((SWEEPS, LANES, 3 * LANES), f32),
            pltpu.VMEM((near_pad * QROWS, LANES), f32),
            pltpu.VMEM((near * QROWS, LANES), f32),
            dma((count,)),
            dma((count,)),
            dma((6,)),
            dma((6,)),
            dma((SWEEPS + 1, 6)),
            dma((SWEEPS + 1, 6)),
            dma((count,)),
            dma((count,)),
        ],
        compiler_params=pltpu.CompilerParams(collective_id=0, has_side_effects=True),
        name="grid",
    )(tile_coords, parts)

    sampled = pl.pallas_call(
        functools.partial(sample_kernel, bins, tpd),
        out_shape=jax.ShapeDtypeStruct((3, bins, points), f32),
        grid_spec=pltpu.PrefetchScalarGridSpec(
            num_scalar_prefetch=3,
            grid=(steps,),
            in_specs=[
                pl.BlockSpec((STEP_BINS, points), rows),
                pl.BlockSpec(((tpd + near) * QROWS, LANES), lambda i, *_: (0, 0)),
            ],
            out_specs=pl.BlockSpec((3, STEP_BINS, points), slabs),
        ),
        compiler_params=pltpu.CompilerParams(dimension_semantics=("arbitrary",)),
        name="sample",
    )(owner_map, bin_tile, bin_count, part_cell, table)
    return velocity, pressure.reshape(-1), jnp.transpose(sampled, (1, 0, 2))


def solution(mesh):
    split_all = AXES
    placed = (
        P(None, split_all),
        P(),
        P(split_all),
        P(split_all),
        P(split_all, None),
        P(split_all, None, None),
        P(split_all, None, None),
        P(split_all, None, None),
        P(split_all, None),
    )
    sizes = tuple(mesh.shape[name] for name in AXES)
    return jax.shard_map(
        functools.partial(local, sizes),
        mesh=mesh,
        in_specs=placed,
        out_specs=(P(None, split_all), P(split_all), P(split_all, None, None)),
        check_vma=False,
    )
```

```python
import functools

import jax
import jax.numpy as jnp
from jax import lax
from jax.experimental import pallas as pl
from jax.experimental.pallas import tpu as pltpu
from jax.sharding import PartitionSpec as P

TILE = 8
SELF_BINS = 32
SWEEPS = 4
CELLS = TILE * TILE * TILE
LANES = 128
GROUPS = CELLS // LANES
QROWS = 4 * GROUPS
BLOCK = QROWS + 8
STEP_BINS = 8
GRAVITY = 0.5
AXES = ("gx", "gy", "gz")
MESH = pl.DeviceIdType.MESH

OFFSETS = [
    (x, y, z)
    for x in (-1, 0, 1)
    for y in (-1, 0, 1)
    for z in (-1, 0, 1)
    if (x, y, z) != (0, 0, 0)
]
FACES = [(1, 0, 0), (-1, 0, 0), (0, 1, 0), (0, -1, 0), (0, 0, 1), (0, 0, -1)]


def lower_hot(cell_row):
    points = cell_row.shape[1]
    low = (cell_row & (LANES - 1)).astype(jnp.float32).astype(jnp.bfloat16)
    rows = lax.broadcasted_iota(jnp.int32, (LANES, points), 0)
    rows = rows.astype(jnp.float32).astype(jnp.bfloat16)
    return jnp.where(rows == low, jnp.bfloat16(1), jnp.bfloat16(0))


def upper_row(cell_row, count):
    lane = lax.broadcasted_iota(jnp.int32, cell_row.shape, 1)
    return jnp.where(lane < count, cell_row >> 7, -1)


def bins_of_step(step, bins, body):
    left = jnp.minimum(STEP_BINS, bins - step * STEP_BINS)
    unroll = 2 if bins % 2 == 0 else 1

    def pair(i, carry):
        for k in range(unroll):
            body(i * unroll + k)
        return carry

    lax.fori_loop(0, left // unroll, pair, 0)


def splat_chunk(start, rows, tpd, owner, tile, count, cell, offset, velocity, affine, mass, out, dep):
    points = cell.shape[1]
    own = pl.ds(start, rows)
    here = pl.ds(0, rows)
    m = mass[own, :]
    dep[0, here, :] = m
    for a in range(3):
        drift = affine[3 * a, own, :] * offset[0, own, :]
        for e in (1, 2):
            drift = drift + affine[3 * a + e, own, :] * offset[e, own, :]
        dep[a + 1, here, :] = m * (velocity[a, own, :] - drift)

    def one(j):
        b = start + j
        cells = cell[pl.ds(b, 1), :]
        upper = upper_row(cells, count[b])
        sub = lax.broadcasted_iota(jnp.int32, (8, points), 0)
        hit = (sub & 3) == upper
        first = sub < 4
        halves = []
        for q in (0, 2):
            both = jnp.where(first, dep[q, pl.ds(j, 1), :], dep[q + 1, pl.ds(j, 1), :])
            halves.append(jnp.where(hit, both, 0.0))
        weighted = jnp.concatenate(halves, axis=0).astype(jnp.bfloat16)
        summed = lax.dot_general(
            weighted,
            lower_hot(cells),
            (((1,), (1,)), ((), ())),
            preferred_element_type=jnp.float32,
        )
        base = pl.multiple_of(b * BLOCK, 8)
        out[pl.ds(base, QROWS), :] = summed
        slot = lax.rem(owner[tile[b]], tpd).astype(jnp.float32)
        out[pl.ds(base + QROWS, 8), :] = jnp.full((8, LANES), slot, jnp.float32)

    unroll = 2 if rows % 2 == 0 else 1

    def pair(i, carry):
        for k in range(unroll):
            one(i * unroll + k)
        return carry

    lax.fori_loop(0, rows // unroll, pair, 0)


def sample_kernel(bins, slots_of, owner, tile, count, cell, table, out):
    step = pl.program_id(0)

    def one(j):
        b = step * STEP_BINS + j
        points = cell.shape[1]
        cells = cell[pl.ds(j, 1), :]
        slot = lax.rem(owner[tile[b]], slots_of)
        place = jnp.where(b < SELF_BINS, slot, slots_of + b - SELF_BINS)
        rows = table[pl.ds(pl.multiple_of(place * QROWS, 8), QROWS), :].astype(jnp.bfloat16)
        planes = lax.dot_general(
            rows, lower_hot(cells), (((1,), (0,)), ((), ())), preferred_element_type=jnp.float32
        )
        upper = upper_row(cells, count[b])
        half = lax.broadcasted_iota(jnp.int32, (8, points), 0) >> 2
        val = jnp.where(upper == half, planes[0:8], 0.0)
        for k in range(1, GROUPS // 2):
            val = val + jnp.where(upper == half + 2 * k, planes[8 * k : 8 * k + 8], 0.0)
        val = val[0:4] + val[4:8]
        for a in range(3):
            out[a, pl.ds(j, 1), :] = val[a : a + 1]

    bins_of_step(step, bins, one)


def split(x):
    high = x.astype(jnp.bfloat16)
    low = (x - high.astype(jnp.float32)).astype(jnp.bfloat16)
    return high, low


def pick(hot, x):
    high, low = split(x)
    return jnp.dot(hot, high, preferred_element_type=jnp.float32) + jnp.dot(
        hot, low, preferred_element_type=jnp.float32
    )


def tile_of(x, u):
    return x[:, u * LANES : (u + 1) * LANES]


def pack_faces(field, axis):
    lane = lax.broadcasted_iota(jnp.int32, (field.shape[0], LANES), 1)
    half = TILE * TILE
    if axis == 0:
        both = jnp.where(lane < half, tile_of(field, 0), tile_of(field, GROUPS - 1))
        return pltpu.roll(both, half, 1)
    stride = (TILE, 1)[axis - 1]
    pos = (lane // stride) % TILE
    packed = jnp.zeros((field.shape[0], LANES), jnp.float32)
    for u in range(GROUPS):
        low = (TILE - 1 - u) * stride
        piece = tile_of(field, u)
        packed = jnp.where(pos == TILE - 1 - u, pltpu.roll(piece, low, 1), packed)
        packed = jnp.where(pos == u, pltpu.roll(piece, LANES - low, 1), packed)
    return packed


def shifted(field, ghost, facing):
    lane = lax.broadcasted_iota(jnp.int32, field.shape, 1)
    stride = (TILE * TILE, TILE, 1)[facing // 2]
    pos = (lane // stride) % TILE
    outer = []
    for u in range(GROUPS):
        move = 0 if facing < 2 else u * stride
        if move and facing % 2:
            move = LANES - move
        outer.append(pltpu.roll(ghost, move, 1) if move else ghost)
    outer = jnp.concatenate(outer, axis=1)
    if facing % 2 == 0:
        return jnp.where(pos == TILE - 1, outer, pltpu.roll(field, CELLS - stride, 1))
    return jnp.where(pos == 0, outer, pltpu.roll(field, stride, 1))


def grid_kernel(
    sizes,
    tpd,
    per,
    near_pad,
    owner,
    tile,
    count,
    coords,
    cell_h,
    offset_h,
    velocity_h,
    affine_h,
    mass_h,
    out_vel,
    out_p,
    out_table,
    cell,
    offset,
    velocity,
    affine,
    mass,
    dep,
    parts,
    load_sem,
    lin_row,
    lins,
    got,
    vel_t,
    p_t,
    reply,
    back,
    part_send,
    part_recv,
    lin_send,
    lin_recv,
    face_send,
    face_recv,
    reply_send,
    reply_recv,
):
    me = [lax.axis_index(name) for name in AXES]
    bins = cell.shape[0]
    chunks = [
        (start, min(STEP_BINS, bins - start))
        for start in [*range(SELF_BINS, bins, STEP_BINS), *range(0, SELF_BINS, STEP_BINS)]
    ]
    loads = []
    for index, (start, rows) in enumerate(chunks):
        span = pl.ds(start, rows)
        sems = iter(range(5))
        loads.append(
            [
                pltpu.make_async_copy(src.at[span], dst.at[span], load_sem.at[index, next(sems)])
                for src, dst in ((cell_h, cell), (mass_h, mass))
            ]
            + [
                pltpu.make_async_copy(
                    src.at[:, span], dst.at[:, span], load_sem.at[index, next(sems)]
                )
                for src, dst in ((offset_h, offset), (velocity_h, velocity), (affine_h, affine))
            ]
        )
        for load in loads[-1]:
            load.start()

    def splat(index):
        for load in loads[index]:
            load.wait()
        start, rows = chunks[index]
        splat_chunk(
            start, rows, tpd, owner, tile, count, cell, offset, velocity, affine, mass, parts, dep
        )

    far_chunks = len(chunks) - SELF_BINS // STEP_BINS

    def inside(rel):
        ok = None
        for n in range(3):
            if rel[n] == 0:
                continue
            one = me[n] < sizes[n] - 1 if rel[n] > 0 else me[n] > 0
            ok = one if ok is None else jnp.logical_and(ok, one)
        return ok

    def at(rel):
        return tuple(
            jnp.clip(me[n] + rel[n], 0, sizes[n] - 1) if rel[n] else me[n] for n in range(3)
        )

    def neg(rel):
        return tuple(-v for v in rel)

    lin = (coords[0:1] * 64 + coords[1:2]) * 64 + coords[2:3]
    lin = jnp.concatenate([lin.astype(jnp.float32)] * (LANES // tpd), axis=1)
    lin_row[...] = jnp.broadcast_to(lin, (8, LANES))
    here = jnp.transpose(jnp.broadcast_to(lin, (LANES, LANES)))[0:tpd]
    lins[...] = jnp.full(lins.shape, -1.0, jnp.float32)
    got[...] = jnp.zeros(got.shape, jnp.float32)
    vel_t[...] = jnp.zeros(vel_t.shape, jnp.float32)
    p_t[...] = jnp.zeros(p_t.shape, jnp.float32)
    back[...] = jnp.zeros(back.shape, jnp.float32)

    barrier = pltpu.get_barrier_semaphore()
    for rel in OFFSETS:

        @pl.when(inside(rel))
        def _(rel=rel):
            pl.semaphore_signal(barrier, inc=1, device_id=at(rel), device_id_type=MESH)

    spans = [
        1 + (me[n] > 0).astype(jnp.int32) + (me[n] < sizes[n] - 1).astype(jnp.int32)
        for n in range(3)
    ]
    for index in range(far_chunks):
        splat(index)
    pl.semaphore_wait(barrier, spans[0] * spans[1] * spans[2] - 1)

    def part_copy(number):
        start = number * per * BLOCK
        rows = (per - 1) * BLOCK + QROWS + 1
        return pltpu.make_async_remote_copy(
            src_ref=parts.at[pl.ds(SELF_BINS * BLOCK + start, rows)],
            dst_ref=got.at[pl.ds(start, rows)],
            send_sem=part_send.at[number],
            recv_sem=part_recv.at[number],
            device_id=at(OFFSETS[number]),
            device_id_type=MESH,
        )

    def reply_copy(number):
        rows = per * QROWS
        return pltpu.make_async_remote_copy(
            src_ref=reply.at[pl.ds(number * rows, rows)],
            dst_ref=back.at[pl.ds(number * rows, rows)],
            send_sem=reply_send.at[number],
            recv_sem=reply_recv.at[number],
            device_id=at(neg(OFFSETS[number])),
            device_id_type=MESH,
        )

    def lin_copy(d, slot):
        return pltpu.make_async_remote_copy(
            src_ref=lin_row,
            dst_ref=lins.at[slot],
            send_sem=lin_send.at[d],
            recv_sem=lin_recv.at[slot],
            device_id=at(FACES[d]),
            device_id_type=MESH,
        )

    def vel_copy(d, slot):
        return pltpu.make_async_remote_copy(
            src_ref=vel_t.at[pl.ds(0, tpd)],
            dst_ref=vel_t.at[pl.ds((1 + slot) * tpd, tpd)],
            send_sem=face_send.at[SWEEPS, d],
            recv_sem=face_recv.at[SWEEPS, slot],
            device_id=at(FACES[d]),
            device_id_type=MESH,
        )

    def p_copy(s):
        def make(d, slot):
            return pltpu.make_async_remote_copy(
                src_ref=p_t.at[s, pl.ds(0, tpd)],
                dst_ref=p_t.at[s, pl.ds((1 + slot) * tpd, tpd)],
                send_sem=face_send.at[s, d],
                recv_sem=face_recv.at[s, slot],
                device_id=at(FACES[d]),
                device_id_type=MESH,
            )

        return make

    def start_faces(make):
        for d in range(6):

            @pl.when(inside(FACES[d]))
            def _(d=d):
                make(d, d ^ 1).start()

    def recv_faces(make):
        for d in range(6):

            @pl.when(inside(FACES[d]))
            def _(d=d):
                make(d, d).wait_recv()

    def sent_faces(make):
        for d in range(6):

            @pl.when(inside(FACES[d]))
            def _(d=d):
                make(d, d ^ 1).wait_send()

    for number, rel in enumerate(OFFSETS):

        @pl.when(inside(rel))
        def _(number=number):
            part_copy(number).start()

    start_faces(lin_copy)
    for index in range(far_chunks, len(chunks)):
        splat(index)

    def hot_of(ref, rows):
        slots = ref[pl.ds(QROWS, rows, stride=BLOCK), :]
        lane = lax.broadcasted_iota(jnp.int32, (rows, LANES), 1).astype(jnp.float32)
        return jnp.where(slots == lane, 1.0, 0.0)

    own_hot = jnp.transpose(hot_of(parts, SELF_BINS))[0:tpd].astype(jnp.bfloat16)
    own = [
        pick(own_hot, parts[pl.ds(r, SELF_BINS, stride=BLOCK), :]) for r in range(QROWS)
    ]
    for number, rel in enumerate(OFFSETS):

        @pl.when(inside(neg(rel)))
        def _(number=number):
            part_copy(number).wait_recv()

    near_hot_t = hot_of(got, near_pad)
    near_hot = jnp.transpose(near_hot_t)[0:tpd].astype(jnp.bfloat16)
    pieces = [
        own[r] + pick(near_hot, got[pl.ds(r, near_pad, stride=BLOCK), :]) for r in range(QROWS)
    ]
    totals = [
        jnp.concatenate(pieces[q * GROUPS : (q + 1) * GROUPS], axis=1) for q in range(4)
    ]
    fluid = totals[0] > 0.0
    safe = jnp.where(fluid, totals[0], 1.0)
    vel = [jnp.where(fluid, totals[1 + a] / safe, 0.0) for a in range(3)]
    vel[1] = vel[1] - GRAVITY * jnp.where(fluid, 1.0, 0.0)
    for a in range(3):
        vel_t[0:tpd, a * LANES : (a + 1) * LANES] = pack_faces(vel[a], a)
    start_faces(vel_copy)

    recv_faces(lin_copy)
    lane = lax.broadcasted_iota(jnp.int32, (8, LANES), 1) // tpd
    cand = jnp.where(lane == 0, lin_row[...], -1.0)
    for d in range(6):
        cand = jnp.where(lane == d + 1, lins[d], cand)
    hots = []
    for face in FACES:
        delta = float((face[0] * 64 + face[1]) * 64 + face[2])
        hots.append(jnp.where(cand[0:1] == here + delta, 1.0, 0.0))

    pair_hots = [
        jnp.concatenate(hots[2 * a : 2 * a + 2], axis=0).astype(jnp.bfloat16) for a in range(3)
    ]
    recv_faces(vel_copy)
    div = None
    for a in range(3):
        ghost = pick(pair_hots[a], vel_t[:, a * LANES : (a + 1) * LANES])
        term = 0.5 * (
            shifted(vel[a], ghost[0:tpd], 2 * a) - shifted(vel[a], ghost[tpd:], 2 * a + 1)
        )
        div = term if div is None else div + term

    press = jnp.where(fluid, (0.0 - div) / 6.0, 0.0)
    for s in range(SWEEPS):
        for a in range(3):
            p_t[s, 0:tpd, a * LANES : (a + 1) * LANES] = pack_faces(press, a)
        start_faces(p_copy(s))
        recv_faces(p_copy(s))
        sides = []
        for a in range(3):
            ghost = pick(pair_hots[a], p_t[s, :, a * LANES : (a + 1) * LANES])
            sides.append(shifted(press, ghost[0:tpd], 2 * a))
            sides.append(shifted(press, ghost[tpd:], 2 * a + 1))
        if s < SWEEPS - 1:
            total = sides[0]
            for d in range(1, 6):
                total = total + sides[d]
            press = jnp.where(fluid, (total - div) / 6.0, 0.0)
    for u in range(GROUPS):
        out_p[pl.ds(u, tpd, stride=GROUPS), :] = press[:, u * LANES : (u + 1) * LANES]
    near_rows = near_hot_t[:, 0:tpd].astype(jnp.bfloat16)
    for a in range(3):
        v = jnp.where(fluid, vel[a] - 0.5 * (sides[2 * a] - sides[2 * a + 1]), 0.0)
        vel[a] = v
        answer = jnp.dot(near_rows, v.astype(jnp.bfloat16), preferred_element_type=jnp.float32)
        for u in range(GROUPS):
            r = 4 * u + a
            reply[pl.ds(r, near_pad, stride=QROWS), :] = answer[:, u * LANES : (u + 1) * LANES]
    for u in range(GROUPS):
        reply[pl.ds(4 * u + 3, near_pad, stride=QROWS), :] = jnp.zeros(
            (near_pad, LANES), jnp.float32
        )
    for number, rel in enumerate(OFFSETS):

        @pl.when(inside(neg(rel)))
        def _(number=number):
            reply_copy(number).start()

    for a in range(3):
        for t in range(tpd):
            out_vel[a : a + 1, t * CELLS : (t + 1) * CELLS] = vel[a][t : t + 1]
        for u in range(GROUPS):
            out_table[pl.ds(4 * u + a, tpd, stride=QROWS), :] = vel[a][
                :, u * LANES : (u + 1) * LANES
            ]
    for u in range(GROUPS):
        out_table[pl.ds(4 * u + 3, tpd, stride=QROWS), :] = jnp.zeros((tpd, LANES), jnp.float32)

    for number, rel in enumerate(OFFSETS):

        @pl.when(inside(rel))
        def _(number=number):
            part_copy(number).wait_send()

    sent_faces(lin_copy)
    sent_faces(vel_copy)
    for s in range(SWEEPS):
        sent_faces(p_copy(s))
    for number, rel in enumerate(OFFSETS):

        @pl.when(inside(rel))
        def _(number=number):
            reply_copy(number).wait_recv()

        @pl.when(inside(neg(rel)))
        def _(number=number):
            reply_copy(number).wait_send()

    near_rows_all = len(OFFSETS) * per * QROWS
    out_table[pl.ds(tpd * QROWS, near_rows_all), :] = back[...]


def local(
    sizes,
    tile_coords,
    owner_map,
    bin_tile,
    bin_count,
    part_cell,
    part_offset,
    part_velocity,
    part_affine,
    part_mass,
):
    tpd = tile_coords.shape[1]
    bins, points = part_cell.shape
    near = bins - SELF_BINS
    per = near // len(OFFSETS)
    near_pad = -(-near // 8) * 8
    steps = -(-bins // STEP_BINS)
    f32 = jnp.float32

    def rows(i, *_):
        return (i, 0)

    def slabs(i, *_):
        return (0, i, 0)

    by_component = [
        jnp.transpose(x, (1, 0, 2)) for x in (part_offset, part_velocity, part_affine)
    ]
    vmem = pl.BlockSpec(memory_space=pltpu.VMEM)
    smem = pl.BlockSpec(memory_space=pltpu.SMEM)
    hbm = pl.BlockSpec(memory_space=pl.ANY)
    dma = pltpu.SemaphoreType.DMA
    count = len(OFFSETS)
    velocity, pressure, table = pl.pallas_call(
        functools.partial(grid_kernel, sizes, tpd, per, near_pad),
        out_shape=(
            jax.ShapeDtypeStruct((3, tpd * CELLS), f32),
            jax.ShapeDtypeStruct((tpd * GROUPS, LANES), f32),
            jax.ShapeDtypeStruct(((tpd + near) * QROWS, LANES), f32),
        ),
        in_specs=[smem] * 3 + [vmem] + [hbm] * 5,
        out_specs=(vmem, vmem, vmem),
        scratch_shapes=[
            pltpu.VMEM((bins, points), jnp.int32),
            pltpu.VMEM((3, bins, points), f32),
            pltpu.VMEM((3, bins, points), f32),
            pltpu.VMEM((9, bins, points), f32),
            pltpu.VMEM((bins, points), f32),
            pltpu.VMEM((4, STEP_BINS, points), f32),
            pltpu.VMEM((bins * BLOCK, LANES), f32),
            dma((steps, 5)),
            pltpu.VMEM((8, LANES), f32),
            pltpu.VMEM((6, 8, LANES), f32),
            pltpu.VMEM((near_pad * BLOCK, LANES), f32),
            pltpu.VMEM((LANES, 3 * LANES), f32),
            pltpu.VMEM((SWEEPS, LANES, 3 * LANES), f32),
            pltpu.VMEM((near_pad * QROWS, LANES), f32),
            pltpu.VMEM((near * QROWS, LANES), f32),
            dma((count,)),
            dma((count,)),
            dma((6,)),
            dma((6,)),
            dma((SWEEPS + 1, 6)),
            dma((SWEEPS + 1, 6)),
            dma((count,)),
            dma((count,)),
        ],
        compiler_params=pltpu.CompilerParams(collective_id=0, has_side_effects=True),
        name="grid",
    )(owner_map, bin_tile, bin_count, tile_coords, part_cell, *by_component, part_mass)

    sampled = pl.pallas_call(
        functools.partial(sample_kernel, bins, tpd),
        out_shape=jax.ShapeDtypeStruct((3, bins, points), f32),
        grid_spec=pltpu.PrefetchScalarGridSpec(
            num_scalar_prefetch=3,
            grid=(steps,),
            in_specs=[
                pl.BlockSpec((STEP_BINS, points), rows),
                pl.BlockSpec(((tpd + near) * QROWS, LANES), lambda i, *_: (0, 0)),
            ],
            out_specs=pl.BlockSpec((3, STEP_BINS, points), slabs),
        ),
        compiler_params=pltpu.CompilerParams(dimension_semantics=("arbitrary",)),
        name="sample",
    )(owner_map, bin_tile, bin_count, part_cell, table)
    return velocity, pressure.reshape(-1), jnp.transpose(sampled, (1, 0, 2))


def solution(mesh):
    split_all = AXES
    placed = (
        P(None, split_all),
        P(),
        P(split_all),
        P(split_all),
        P(split_all, None),
        P(split_all, None, None),
        P(split_all, None, None),
        P(split_all, None, None),
        P(split_all, None),
    )
    sizes = tuple(mesh.shape[name] for name in AXES)
    return jax.shard_map(
        functools.partial(local, sizes),
        mesh=mesh,
        in_specs=placed,
        out_specs=(P(None, split_all), P(split_all), P(split_all, None, None)),
        check_vma=False,
    )
```

```python
import functools

import jax
import jax.numpy as jnp
from jax import lax
from jax.experimental import pallas as pl
from jax.experimental.pallas import tpu as pltpu
from jax.sharding import PartitionSpec as P

TILE = 8
SELF_BINS = 32
SWEEPS = 4
CELLS = TILE * TILE * TILE
LANES = 128
GROUPS = CELLS // LANES
QROWS = 4 * GROUPS
BLOCK = QROWS + 8
STEP_BINS = 8
GRAVITY = 0.5
AXES = ("gx", "gy", "gz")
MESH = pl.DeviceIdType.MESH

OFFSETS = [
    (x, y, z)
    for x in (-1, 0, 1)
    for y in (-1, 0, 1)
    for z in (-1, 0, 1)
    if (x, y, z) != (0, 0, 0)
]
FACES = [(1, 0, 0), (-1, 0, 0), (0, 1, 0), (0, -1, 0), (0, 0, 1), (0, 0, -1)]


def lower_hot(cell_row):
    points = cell_row.shape[1]
    low = (cell_row & (LANES - 1)).astype(jnp.float32).astype(jnp.bfloat16)
    rows = lax.broadcasted_iota(jnp.int32, (LANES, points), 0)
    rows = rows.astype(jnp.float32).astype(jnp.bfloat16)
    return jnp.where(rows == low, jnp.bfloat16(1), jnp.bfloat16(0))


def upper_row(cell_row, count):
    lane = lax.broadcasted_iota(jnp.int32, cell_row.shape, 1)
    return jnp.where(lane < count, cell_row >> 7, -1)


def unrolled(rows, body):
    unroll = next(n for n in (4, 2, 1) if rows % n == 0)

    def group(i, carry):
        for k in range(unroll):
            body(i * unroll + k)
        return carry

    lax.fori_loop(0, rows // unroll, group, 0)


def bins_of_step(step, bins, body):
    tail = bins % STEP_BINS
    full = bins // STEP_BINS

    @pl.when(step < full)
    def _():
        unrolled(STEP_BINS, body)

    if tail:

        @pl.when(step == full)
        def _():
            unrolled(tail, body)


def splat_chunk(start, rows, tpd, owner, tile, count, cell, offset, velocity, affine, mass, out, dep):
    points = cell.shape[1]
    own = pl.ds(start, rows)
    here = pl.ds(0, rows)
    m = mass[own, :]
    dep[0, here, :] = m
    for a in range(3):
        drift = affine[3 * a, own, :] * offset[0, own, :]
        for e in (1, 2):
            drift = drift + affine[3 * a + e, own, :] * offset[e, own, :]
        dep[a + 1, here, :] = m * (velocity[a, own, :] - drift)

    def one(j):
        b = start + j
        cells = cell[pl.ds(b, 1), :]
        upper = upper_row(cells, count[b])
        sub = lax.broadcasted_iota(jnp.int32, (8, points), 0)
        hit = (sub & 3) == upper
        first = sub < 4
        halves = []
        for q in (0, 2):
            both = jnp.where(first, dep[q, pl.ds(j, 1), :], dep[q + 1, pl.ds(j, 1), :])
            halves.append(jnp.where(hit, both, 0.0))
        weighted = jnp.concatenate(halves, axis=0).astype(jnp.bfloat16)
        summed = lax.dot_general(
            weighted,
            lower_hot(cells),
            (((1,), (1,)), ((), ())),
            preferred_element_type=jnp.float32,
        )
        base = pl.multiple_of(b * BLOCK, 8)
        out[pl.ds(base, QROWS), :] = summed
        slot = lax.rem(owner[tile[b]], tpd).astype(jnp.float32)
        out[pl.ds(base + QROWS, 8), :] = jnp.full((8, LANES), slot, jnp.float32)

    unrolled(rows, one)


def sample_kernel(bins, slots_of, owner, tile, count, cell, table, out):
    step = pl.program_id(0)

    def one(j):
        b = step * STEP_BINS + j
        points = cell.shape[1]
        cells = cell[pl.ds(j, 1), :]
        slot = lax.rem(owner[tile[b]], slots_of)
        place = jnp.where(b < SELF_BINS, slot, slots_of + b - SELF_BINS)
        rows = table[pl.ds(pl.multiple_of(place * QROWS, 8), QROWS), :].astype(jnp.bfloat16)
        planes = lax.dot_general(
            rows, lower_hot(cells), (((1,), (0,)), ((), ())), preferred_element_type=jnp.float32
        )
        upper = upper_row(cells, count[b])
        half = lax.broadcasted_iota(jnp.int32, (8, points), 0) >> 2
        val = jnp.where(upper == half, planes[0:8], 0.0)
        for k in range(1, GROUPS // 2):
            val = val + jnp.where(upper == half + 2 * k, planes[8 * k : 8 * k + 8], 0.0)
        val = val[0:4] + val[4:8]
        for a in range(3):
            out[a, pl.ds(j, 1), :] = val[a : a + 1]

    bins_of_step(step, bins, one)


def split(x):
    high = x.astype(jnp.bfloat16)
    low = (x - high.astype(jnp.float32)).astype(jnp.bfloat16)
    return high, low


def pick(hot, x):
    high, low = split(x)
    return jnp.dot(hot, high, preferred_element_type=jnp.float32) + jnp.dot(
        hot, low, preferred_element_type=jnp.float32
    )


def tile_of(x, u):
    return x[:, u * LANES : (u + 1) * LANES]


def pack_faces(field, axis):
    lane = lax.broadcasted_iota(jnp.int32, (field.shape[0], LANES), 1)
    half = TILE * TILE
    if axis == 0:
        both = jnp.where(lane < half, tile_of(field, 0), tile_of(field, GROUPS - 1))
        return pltpu.roll(both, half, 1)
    stride = (TILE, 1)[axis - 1]
    pos = (lane // stride) % TILE
    packed = jnp.zeros((field.shape[0], LANES), jnp.float32)
    for u in range(GROUPS):
        low = (TILE - 1 - u) * stride
        piece = tile_of(field, u)
        packed = jnp.where(pos == TILE - 1 - u, pltpu.roll(piece, low, 1), packed)
        packed = jnp.where(pos == u, pltpu.roll(piece, LANES - low, 1), packed)
    return packed


def shifted(field, ghost, facing):
    lane = lax.broadcasted_iota(jnp.int32, field.shape, 1)
    stride = (TILE * TILE, TILE, 1)[facing // 2]
    pos = (lane // stride) % TILE
    outer = []
    for u in range(GROUPS):
        move = 0 if facing < 2 else u * stride
        if move and facing % 2:
            move = LANES - move
        outer.append(pltpu.roll(ghost, move, 1) if move else ghost)
    outer = jnp.concatenate(outer, axis=1)
    if facing % 2 == 0:
        return jnp.where(pos == TILE - 1, outer, pltpu.roll(field, CELLS - stride, 1))
    return jnp.where(pos == 0, outer, pltpu.roll(field, stride, 1))


def grid_kernel(
    sizes,
    tpd,
    per,
    near_pad,
    owner,
    tile,
    count,
    coords,
    cell_h,
    offset_h,
    velocity_h,
    affine_h,
    mass_h,
    out_vel,
    out_p,
    out_table,
    cell,
    offset,
    velocity,
    affine,
    mass,
    dep,
    parts,
    load_sem,
    lin_row,
    lins,
    got,
    vel_t,
    p_t,
    reply,
    back,
    part_send,
    part_recv,
    lin_send,
    lin_recv,
    face_send,
    face_recv,
    reply_send,
    reply_recv,
):
    me = [lax.axis_index(name) for name in AXES]
    bins = cell.shape[0]
    chunks = [
        (start, min(STEP_BINS, bins - start))
        for start in [*range(SELF_BINS, bins, STEP_BINS), *range(0, SELF_BINS, STEP_BINS)]
    ]
    loads = []
    for index, (start, rows) in enumerate(chunks):
        span = pl.ds(start, rows)
        sems = iter(range(5))
        loads.append(
            [
                pltpu.make_async_copy(src.at[span], dst.at[span], load_sem.at[index, next(sems)])
                for src, dst in ((cell_h, cell), (mass_h, mass))
            ]
            + [
                pltpu.make_async_copy(
                    src.at[:, span], dst.at[:, span], load_sem.at[index, next(sems)]
                )
                for src, dst in ((offset_h, offset), (velocity_h, velocity), (affine_h, affine))
            ]
        )
        for load in loads[-1]:
            load.start()

    def splat(index):
        for load in loads[index]:
            load.wait()
        start, rows = chunks[index]
        splat_chunk(
            start, rows, tpd, owner, tile, count, cell, offset, velocity, affine, mass, parts, dep
        )

    far_chunks = len(chunks) - SELF_BINS // STEP_BINS

    def inside(rel):
        ok = None
        for n in range(3):
            if rel[n] == 0:
                continue
            one = me[n] < sizes[n] - 1 if rel[n] > 0 else me[n] > 0
            ok = one if ok is None else jnp.logical_and(ok, one)
        return ok

    def at(rel):
        return tuple(
            jnp.clip(me[n] + rel[n], 0, sizes[n] - 1) if rel[n] else me[n] for n in range(3)
        )

    def neg(rel):
        return tuple(-v for v in rel)

    lin = (coords[0:1] * 64 + coords[1:2]) * 64 + coords[2:3]
    lin = jnp.concatenate([lin.astype(jnp.float32)] * (LANES // tpd), axis=1)
    lin_row[...] = jnp.broadcast_to(lin, (8, LANES))
    here = jnp.transpose(jnp.broadcast_to(lin, (LANES, LANES)))[0:tpd]
    lins[...] = jnp.full(lins.shape, -1.0, jnp.float32)
    got[...] = jnp.zeros(got.shape, jnp.float32)
    vel_t[...] = jnp.zeros(vel_t.shape, jnp.float32)
    p_t[...] = jnp.zeros(p_t.shape, jnp.float32)
    back[...] = jnp.zeros(back.shape, jnp.float32)

    barrier = pltpu.get_barrier_semaphore()
    for rel in OFFSETS:

        @pl.when(inside(rel))
        def _(rel=rel):
            pl.semaphore_signal(barrier, inc=1, device_id=at(rel), device_id_type=MESH)

    spans = [
        1 + (me[n] > 0).astype(jnp.int32) + (me[n] < sizes[n] - 1).astype(jnp.int32)
        for n in range(3)
    ]
    for index in range(far_chunks):
        splat(index)
    pl.semaphore_wait(barrier, spans[0] * spans[1] * spans[2] - 1)

    def part_copy(number):
        start = number * per * BLOCK
        rows = (per - 1) * BLOCK + QROWS + 1
        return pltpu.make_async_remote_copy(
            src_ref=parts.at[pl.ds(SELF_BINS * BLOCK + start, rows)],
            dst_ref=got.at[pl.ds(start, rows)],
            send_sem=part_send.at[number],
            recv_sem=part_recv.at[number],
            device_id=at(OFFSETS[number]),
            device_id_type=MESH,
        )

    def reply_copy(number):
        rows = per * QROWS
        return pltpu.make_async_remote_copy(
            src_ref=reply.at[pl.ds(number * rows, rows)],
            dst_ref=back.at[pl.ds(number * rows, rows)],
            send_sem=reply_send.at[number],
            recv_sem=reply_recv.at[number],
            device_id=at(neg(OFFSETS[number])),
            device_id_type=MESH,
        )

    def lin_copy(d, slot):
        return pltpu.make_async_remote_copy(
            src_ref=lin_row,
            dst_ref=lins.at[slot],
            send_sem=lin_send.at[d],
            recv_sem=lin_recv.at[slot],
            device_id=at(FACES[d]),
            device_id_type=MESH,
        )

    def vel_copy(d, slot):
        return pltpu.make_async_remote_copy(
            src_ref=vel_t.at[pl.ds(0, tpd)],
            dst_ref=vel_t.at[pl.ds((1 + slot) * tpd, tpd)],
            send_sem=face_send.at[SWEEPS, d],
            recv_sem=face_recv.at[SWEEPS, slot],
            device_id=at(FACES[d]),
            device_id_type=MESH,
        )

    def p_copy(s):
        def make(d, slot):
            return pltpu.make_async_remote_copy(
                src_ref=p_t.at[s, pl.ds(0, tpd)],
                dst_ref=p_t.at[s, pl.ds((1 + slot) * tpd, tpd)],
                send_sem=face_send.at[s, d],
                recv_sem=face_recv.at[s, slot],
                device_id=at(FACES[d]),
                device_id_type=MESH,
            )

        return make

    def start_faces(make):
        for d in range(6):

            @pl.when(inside(FACES[d]))
            def _(d=d):
                make(d, d ^ 1).start()

    def recv_faces(make):
        for d in range(6):

            @pl.when(inside(FACES[d]))
            def _(d=d):
                make(d, d).wait_recv()

    def sent_faces(make):
        for d in range(6):

            @pl.when(inside(FACES[d]))
            def _(d=d):
                make(d, d ^ 1).wait_send()

    for number, rel in enumerate(OFFSETS):

        @pl.when(inside(rel))
        def _(number=number):
            part_copy(number).start()

    start_faces(lin_copy)
    for index in range(far_chunks, len(chunks)):
        splat(index)

    def hot_of(ref, rows):
        slots = ref[pl.ds(QROWS, rows, stride=BLOCK), :]
        lane = lax.broadcasted_iota(jnp.int32, (rows, LANES), 1).astype(jnp.float32)
        return jnp.where(slots == lane, 1.0, 0.0)

    own_hot = jnp.transpose(hot_of(parts, SELF_BINS))[0:tpd].astype(jnp.bfloat16)
    own = [
        pick(own_hot, parts[pl.ds(r, SELF_BINS, stride=BLOCK), :]) for r in range(QROWS)
    ]
    for number, rel in enumerate(OFFSETS):

        @pl.when(inside(neg(rel)))
        def _(number=number):
            part_copy(number).wait_recv()

    near_hot_t = hot_of(got, near_pad)
    near_hot = jnp.transpose(near_hot_t)[0:tpd].astype(jnp.bfloat16)
    pieces = [
        own[r] + pick(near_hot, got[pl.ds(r, near_pad, stride=BLOCK), :]) for r in range(QROWS)
    ]
    totals = [
        jnp.concatenate(pieces[q * GROUPS : (q + 1) * GROUPS], axis=1) for q in range(4)
    ]
    fluid = totals[0] > 0.0
    safe = jnp.where(fluid, totals[0], 1.0)
    vel = [jnp.where(fluid, totals[1 + a] / safe, 0.0) for a in range(3)]
    vel[1] = vel[1] - GRAVITY * jnp.where(fluid, 1.0, 0.0)
    for a in range(3):
        vel_t[0:tpd, a * LANES : (a + 1) * LANES] = pack_faces(vel[a], a)
    start_faces(vel_copy)

    recv_faces(lin_copy)
    lane = lax.broadcasted_iota(jnp.int32, (8, LANES), 1) // tpd
    cand = jnp.where(lane == 0, lin_row[...], -1.0)
    for d in range(6):
        cand = jnp.where(lane == d + 1, lins[d], cand)
    hots = []
    for face in FACES:
        delta = float((face[0] * 64 + face[1]) * 64 + face[2])
        hots.append(jnp.where(cand[0:1] == here + delta, 1.0, 0.0))

    pair_hots = [
        jnp.concatenate(hots[2 * a : 2 * a + 2], axis=0).astype(jnp.bfloat16) for a in range(3)
    ]
    recv_faces(vel_copy)
    div = None
    for a in range(3):
        ghost = pick(pair_hots[a], vel_t[:, a * LANES : (a + 1) * LANES])
        term = 0.5 * (
            shifted(vel[a], ghost[0:tpd], 2 * a) - shifted(vel[a], ghost[tpd:], 2 * a + 1)
        )
        div = term if div is None else div + term

    press = jnp.where(fluid, (0.0 - div) / 6.0, 0.0)
    for s in range(SWEEPS):
        for a in range(3):
            p_t[s, 0:tpd, a * LANES : (a + 1) * LANES] = pack_faces(press, a)
        start_faces(p_copy(s))
        recv_faces(p_copy(s))
        sides = []
        for a in range(3):
            ghost = pick(pair_hots[a], p_t[s, :, a * LANES : (a + 1) * LANES])
            sides.append(shifted(press, ghost[0:tpd], 2 * a))
            sides.append(shifted(press, ghost[tpd:], 2 * a + 1))
        if s < SWEEPS - 1:
            total = sides[0]
            for d in range(1, 6):
                total = total + sides[d]
            press = jnp.where(fluid, (total - div) / 6.0, 0.0)
    for u in range(GROUPS):
        out_p[pl.ds(u, tpd, stride=GROUPS), :] = press[:, u * LANES : (u + 1) * LANES]
    near_rows = near_hot_t[:, 0:tpd].astype(jnp.bfloat16)
    for a in range(3):
        v = jnp.where(fluid, vel[a] - 0.5 * (sides[2 * a] - sides[2 * a + 1]), 0.0)
        vel[a] = v
        answer = jnp.dot(near_rows, v.astype(jnp.bfloat16), preferred_element_type=jnp.float32)
        for u in range(GROUPS):
            r = 4 * u + a
            reply[pl.ds(r, near_pad, stride=QROWS), :] = answer[:, u * LANES : (u + 1) * LANES]
    for u in range(GROUPS):
        reply[pl.ds(4 * u + 3, near_pad, stride=QROWS), :] = jnp.zeros(
            (near_pad, LANES), jnp.float32
        )
    for number, rel in enumerate(OFFSETS):

        @pl.when(inside(neg(rel)))
        def _(number=number):
            reply_copy(number).start()

    for a in range(3):
        for t in range(tpd):
            out_vel[a : a + 1, t * CELLS : (t + 1) * CELLS] = vel[a][t : t + 1]
        for u in range(GROUPS):
            out_table[pl.ds(4 * u + a, tpd, stride=QROWS), :] = vel[a][
                :, u * LANES : (u + 1) * LANES
            ]
    for u in range(GROUPS):
        out_table[pl.ds(4 * u + 3, tpd, stride=QROWS), :] = jnp.zeros((tpd, LANES), jnp.float32)

    for number, rel in enumerate(OFFSETS):

        @pl.when(inside(rel))
        def _(number=number):
            part_copy(number).wait_send()

    sent_faces(lin_copy)
    sent_faces(vel_copy)
    for s in range(SWEEPS):
        sent_faces(p_copy(s))
    for number, rel in enumerate(OFFSETS):

        @pl.when(inside(rel))
        def _(number=number):
            reply_copy(number).wait_recv()

        @pl.when(inside(neg(rel)))
        def _(number=number):
            reply_copy(number).wait_send()

    near_rows_all = len(OFFSETS) * per * QROWS
    out_table[pl.ds(tpd * QROWS, near_rows_all), :] = back[...]


def local(
    sizes,
    tile_coords,
    owner_map,
    bin_tile,
    bin_count,
    part_cell,
    part_offset,
    part_velocity,
    part_affine,
    part_mass,
):
    tpd = tile_coords.shape[1]
    bins, points = part_cell.shape
    near = bins - SELF_BINS
    per = near // len(OFFSETS)
    near_pad = -(-near // 8) * 8
    steps = -(-bins // STEP_BINS)
    f32 = jnp.float32

    def rows(i, *_):
        return (i, 0)

    def slabs(i, *_):
        return (0, i, 0)

    by_component = [
        jnp.transpose(x, (1, 0, 2)) for x in (part_offset, part_velocity, part_affine)
    ]
    vmem = pl.BlockSpec(memory_space=pltpu.VMEM)
    smem = pl.BlockSpec(memory_space=pltpu.SMEM)
    hbm = pl.BlockSpec(memory_space=pl.ANY)
    dma = pltpu.SemaphoreType.DMA
    count = len(OFFSETS)
    velocity, pressure, table = pl.pallas_call(
        functools.partial(grid_kernel, sizes, tpd, per, near_pad),
        out_shape=(
            jax.ShapeDtypeStruct((3, tpd * CELLS), f32),
            jax.ShapeDtypeStruct((tpd * GROUPS, LANES), f32),
            jax.ShapeDtypeStruct(((tpd + near) * QROWS, LANES), f32),
        ),
        in_specs=[smem] * 3 + [vmem] + [hbm] * 5,
        out_specs=(vmem, vmem, vmem),
        scratch_shapes=[
            pltpu.VMEM((bins, points), jnp.int32),
            pltpu.VMEM((3, bins, points), f32),
            pltpu.VMEM((3, bins, points), f32),
            pltpu.VMEM((9, bins, points), f32),
            pltpu.VMEM((bins, points), f32),
            pltpu.VMEM((4, STEP_BINS, points), f32),
            pltpu.VMEM((bins * BLOCK, LANES), f32),
            dma((steps, 5)),
            pltpu.VMEM((8, LANES), f32),
            pltpu.VMEM((6, 8, LANES), f32),
            pltpu.VMEM((near_pad * BLOCK, LANES), f32),
            pltpu.VMEM((LANES, 3 * LANES), f32),
            pltpu.VMEM((SWEEPS, LANES, 3 * LANES), f32),
            pltpu.VMEM((near_pad * QROWS, LANES), f32),
            pltpu.VMEM((near * QROWS, LANES), f32),
            dma((count,)),
            dma((count,)),
            dma((6,)),
            dma((6,)),
            dma((SWEEPS + 1, 6)),
            dma((SWEEPS + 1, 6)),
            dma((count,)),
            dma((count,)),
        ],
        compiler_params=pltpu.CompilerParams(collective_id=0, has_side_effects=True),
        name="grid",
    )(owner_map, bin_tile, bin_count, tile_coords, part_cell, *by_component, part_mass)

    sampled = pl.pallas_call(
        functools.partial(sample_kernel, bins, tpd),
        out_shape=jax.ShapeDtypeStruct((3, bins, points), f32),
        grid_spec=pltpu.PrefetchScalarGridSpec(
            num_scalar_prefetch=3,
            grid=(steps,),
            in_specs=[
                pl.BlockSpec((STEP_BINS, points), rows),
                pl.BlockSpec(((tpd + near) * QROWS, LANES), lambda i, *_: (0, 0)),
            ],
            out_specs=pl.BlockSpec((3, STEP_BINS, points), slabs),
        ),
        compiler_params=pltpu.CompilerParams(dimension_semantics=("arbitrary",)),
        name="sample",
    )(owner_map, bin_tile, bin_count, part_cell, table)
    return velocity, pressure.reshape(-1), jnp.transpose(sampled, (1, 0, 2))


def solution(mesh):
    split_all = AXES
    placed = (
        P(None, split_all),
        P(),
        P(split_all),
        P(split_all),
        P(split_all, None),
        P(split_all, None, None),
        P(split_all, None, None),
        P(split_all, None, None),
        P(split_all, None),
    )
    sizes = tuple(mesh.shape[name] for name in AXES)
    return jax.shard_map(
        functools.partial(local, sizes),
        mesh=mesh,
        in_specs=placed,
        out_specs=(P(None, split_all), P(split_all), P(split_all, None, None)),
        check_vma=False,
    )
```
